256 devices in a mesh: frames: 64 (over z, x, core), centers: 4 (over y).
Axes of the slice: x: 4, y: 4, z: 8, core: 2. Of those that a mesh axis runs over, the one named last changes fastest.
Arguments:
- frames: bfloat16 [65536, 512], P('frames'), may hold values from -24 to 24
- centers: bfloat16 [16384, 512], P('centers'), may hold values from -6 to 6
- starts: int32 [64], replicated, may hold values from 0 to 65535, as said below
Outputs:
- counts: float32 [512, 16384], P('frames', 'centers')
The draws below stay inside these ranges and needn't reach their ends.
Inputs may be any that keep to these rules, and one draw needn't show every extreme that they name: starts[0] is 0 and the entries rise strictly.
All inputs are finite; a program needn't handle non-finite values.
Results may differ from the reference program's by a relative error of at most 0.001.
Values may be sent and summed in bfloat16 or wider, within the bound.
No kernel may reach another device: no remote copies, remote signals or barrier semaphores. Data moves between devices by JAX's collectives and lax.ppermute only.
A program may use at most 128 MiB of HBM per device.

```python
import jax
import jax.numpy as jnp
from jax import lax

D = 512
K = 16384
W = 512
LAG = 5
F_DEV = 1024
NSEG = 64
NF = 65536


def draw_frames(key, part):
    base = jax.random.normal(key, (NF, D), jnp.float32)
    base = jnp.clip(base, -6.0, 6.0)
    chosen = jax.random.uniform(jax.random.fold_in(key, 11), (NF, 1), jnp.float32) < 0.03125
    level = jax.random.randint(jax.random.fold_in(key, 13), (NF, 1), 0, 3).astype(jnp.float32)
    flip = jax.random.uniform(jax.random.fold_in(key, 17), (NF, 1), jnp.float32) < 0.5
    offset = (12.0 + 4.0 * level) * jnp.where(flip, -1.0, 1.0)
    base = jnp.clip(base + jnp.where(chosen, offset, 0.0), -24.0, 24.0)
    return base.astype(jnp.bfloat16)


def draw_starts(key, part):
    picks = jax.random.permutation(key, NF - 1)[:NSEG - 1] + 1
    return jnp.concatenate([jnp.zeros((1,), jnp.int32), jnp.sort(picks).astype(jnp.int32)])


def block_scale(own_key, extent, shards, low, largest):
    factor_of = 1.0
    for dim, shards_of in shards:
        draws = jax.random.uniform(jax.random.fold_in(jax.random.fold_in(own_key, 6), dim), (shards_of,), jnp.float32, low / len(shards), largest / len(shards))
        factor_of = factor_of * jnp.repeat(jnp.exp(draws), extent[dim] // shards_of).reshape((-1,) + (1,) * (len(extent) - 1 - dim))
    return factor_of


def bell_draw(key, shape, width, most, shards=(), held_as=jnp.bfloat16):
    values = jax.random.normal(key, shape, jnp.float32) * width
    if len(shards) > 0:
        values = block_scale(key, shape, shards, -0.22, 0.18) * values
    return jnp.clip(values, min=-most, max=most).astype(held_as)


def setup_inputs(seed: int = 0) -> dict:
    seeds = jax.random.split(jax.random.key(seed), 4)
    return {
        "frames": draw_frames(jax.random.fold_in(seeds[3], 71), 0),
        "centers": bell_draw(seeds[1], (K, D), 1.0, 6.0, ((0, 4),)),
        "starts": draw_starts(jax.random.fold_in(seeds[3], 71), 0),
    }


SHARPNESS = 0.03125


def logits_of(row_block, centers):
    inner_prod = jnp.dot(row_block, centers.T, preferred_element_type=jnp.float32)
    frame_norm = jnp.sum(row_block.astype(jnp.float32) ** 2, axis=1, keepdims=True)
    center_norm = jnp.sum(centers.astype(jnp.float32) ** 2, axis=1)
    return -SHARPNESS * (frame_norm - 2.0 * inner_prod + center_norm[None, :])


def segment_of(positions, starts):
    return jnp.sum((starts[None, :] <= positions[:, None]).astype(jnp.int32), axis=1)


def pair_mask(positions, starts):
    later = positions + LAG
    same = segment_of(positions, starts) == segment_of(later, starts)
    return jnp.logical_and(same, later < NF)


def reference(frames, centers, starts):
    padded = jnp.concatenate([frames, jnp.zeros((LAG, D), frames.dtype)], axis=0)

    def block(accumulated, block_index):
        first_frame = block_index * F_DEV
        row_block = lax.dynamic_slice_in_dim(padded, first_frame, F_DEV + LAG, 0)
        logits = logits_of(row_block, centers)
        row_top = jnp.max(logits, axis=1, keepdims=True)
        exponent = jnp.exp(logits - row_top)
        member = (exponent / jnp.sum(exponent, axis=1, keepdims=True)).astype(jnp.bfloat16)
        positions = first_frame + jnp.arange(F_DEV, dtype=jnp.int32)
        usable = pair_mask(positions, starts)
        lead_rows = member[:F_DEV, :W] * usable[:, None].astype(jnp.bfloat16)
        lag_rows = member[LAG:, :]
        partial_value = lax.dot_general(lead_rows, lag_rows, (((0,), (0,)), ((), ())), preferred_element_type=jnp.float32)
        return accumulated + partial_value, None

    counts, _ = lax.scan(block, jnp.zeros((W, K), jnp.float32), jnp.arange(NF // F_DEV, dtype=jnp.int32))
    return counts * (K * K / NF)
```

```python
import math

import jax
import jax.numpy as jnp
from jax import lax
from jax.experimental import pallas as pl
from jax.experimental.pallas import tpu as pltpu
from jax.sharding import Mesh, PartitionSpec as P

K = 16384
W = 512
LAG = 5
D = 512
SHARPNESS = 0.03125

NZ, NX, NC, NY = 8, 4, 2, 4
F = 1024
FC = NC * F
TAIL = 128
FE = TAIL + FC
KD = 2048
FB = 256
KB = 256
NB = FC // FB
CH = W // NX
HALF = KD // 2

LOG2E = math.log2(math.e)
GAIN = 2.0 * SHARPNESS * LOG2E
NORM = -SHARPNESS * LOG2E


NT = (((1,), (1,)), ((), ()))


def member_kernel(core, own, partner, tail, centers, e_ref, st_ref, peers_ref, xs, cs, bias, u, sems):
    c = core[0]
    copies = [
        pltpu.make_async_copy(centers.at[pl.ds(c * KD, KD)], cs, sems.at[0]),
        pltpu.make_async_copy(own, xs.at[pl.ds(TAIL + c * F, F)], sems.at[1]),
        pltpu.make_async_copy(partner, xs.at[pl.ds(TAIL + (1 - c) * F, F)], sems.at[2]),
        pltpu.make_async_copy(tail, xs.at[pl.ds(0, TAIL)], sems.at[3]),
    ]
    for copy in copies:
        copy.start()
    for copy in copies:
        copy.wait()

    for i in range(KD // KB):
        block = cs[i * KB:(i + 1) * KB, :].astype(jnp.float32)
        norm = jnp.sum(block * block, axis=1, keepdims=True)
        bias[i * KB:(i + 1) * KB, :] = jnp.broadcast_to(NORM * norm, (KB, 128))

    def frame_block(start, width, keep):
        xb = xs[pl.ds(start, width), :]
        xf = xb.astype(jnp.float32)
        sq = xf * xf
        part = sq[:, 0:128] + sq[:, 128:256] + sq[:, 256:384] + sq[:, 384:512]
        frame = NORM * jnp.sum(part.T, axis=0, keepdims=True)
        highest = None
        for i in range(KD // KB):
            ip = lax.dot_general(cs[i * KB:(i + 1) * KB, :], xb, NT, preferred_element_type=jnp.float32)
            b = bias[i * KB:(i + 1) * KB, :]
            v = ip * GAIN + (b if width == 128 else jnp.concatenate([b] * (width // 128), axis=1))
            u[i * KB:(i + 1) * KB, 0:width] = v
            h = jnp.max(v.reshape(KB // 8, 8, width), axis=0)
            highest = h if highest is None else jnp.maximum(highest, h)
        top = jnp.max(highest, axis=0, keepdims=True) + frame
        shift = frame - top
        total = None
        for i in range(KD // KB):
            e = jnp.exp2(u[i * KB:(i + 1) * KB, 0:width] + shift)
            s = jnp.sum(e.reshape(KB // 8, 8, width), axis=0)
            total = s if total is None else total + s
            if keep:
                e_ref[i * KB:(i + 1) * KB, pl.ds(start - TAIL, width)] = e.astype(jnp.bfloat16)
        total = jnp.sum(total, axis=0, keepdims=True)
        st_ref[0:1, pl.ds(start, width)] = top
        st_ref[1:2, pl.ds(start, width)] = frame
        both = jnp.concatenate([top, total], axis=0)
        peers_ref[:, :, pl.ds(start, width)] = jnp.broadcast_to(both[None], (NC * NY, 2, width))

    frame_block(0, TAIL, False)

    def step(b, carry):
        frame_block(pl.multiple_of(TAIL + b * FB, 128), FB, True)
        return carry

    lax.fori_loop(0, NB, step, 0)


def memberships(core, own, partner, tail, centers):
    anyspace = pl.BlockSpec(memory_space=pl.ANY)
    vmem = pl.BlockSpec(memory_space=pltpu.VMEM)
    return pl.pallas_call(
        member_kernel,
        in_specs=[pl.BlockSpec(memory_space=pltpu.SMEM)] + [anyspace] * 4,
        out_specs=[vmem, vmem, vmem],
        out_shape=[
            jax.ShapeDtypeStruct((KD, FC), jnp.bfloat16),
            jax.ShapeDtypeStruct((2, FE), jnp.float32),
            jax.ShapeDtypeStruct((NC * NY, 2, FE), jnp.float32),
        ],
        scratch_shapes=[
            pltpu.VMEM((FE, D), jnp.bfloat16),
            pltpu.VMEM((KD, D), jnp.bfloat16),
            pltpu.VMEM((KD, 128), jnp.float32),
            pltpu.VMEM((KD, FB), jnp.float32),
            pltpu.SemaphoreType.DMA((4,)),
        ],
        name="memberships",
    )(core, own, partner, tail, centers)


def count_kernel(where, own, partner, tail, window, mine, peers, usable, e_ref,
                 a2, b2, pa, pb, ma, mb, home, xs, lead, sems):
    c = where[0]
    x = where[1]
    j = pl.program_id(0)

    @pl.when(j == 0)
    def _():
        copies = [
            pltpu.make_async_copy(own, xs.at[pl.ds(TAIL + c * F, F)], sems.at[0]),
            pltpu.make_async_copy(partner, xs.at[pl.ds(TAIL + (1 - c) * F, F)], sems.at[1]),
            pltpu.make_async_copy(tail, xs.at[pl.ds(0, TAIL)], sems.at[2]),
        ]
        for copy in copies:
            copy.start()
        tops = peers[:, 0, :]
        top = jnp.max(tops, axis=0, keepdims=True)
        total = jnp.sum(peers[:, 1, :] * jnp.exp2(tops - top), axis=0, keepdims=True)
        inverse = 1.0 / total
        lag_side = usable[...] * jnp.exp2(mine[0:1, :] - top) * inverse
        shift = mine[1:2, :] - top
        scale = inverse * pltpu.roll(lag_side, FE - LAG, 1)
        for copy in copies:
            copy.wait()
        for d in range(NX):
            rows = window[:, lax.rem(x + d, NX), :, :].reshape(CH, D)
            rf = rows.astype(jnp.float32)
            bias = NORM * jnp.sum(rf * rf, axis=1, keepdims=True)
            ip = lax.dot_general(rows, xs[...], NT, preferred_element_type=jnp.float32)
            m = jnp.exp2(ip * GAIN + bias + shift) * scale
            lead[d * CH:(d + 1) * CH, :] = pltpu.roll(m, LAG, 1)[:, TAIL:].astype(jnp.bfloat16)

    part = lax.dot_general(lead[...], e_ref[...], NT, preferred_element_type=jnp.float32)
    home[...] = part[0:CH]
    bf = jnp.bfloat16

    @pl.when(j < NB // 2)
    def _():
        pa[...] = part[CH:2 * CH]
        a2[...] = part[2 * CH:3 * CH].astype(bf)
        ma[...] = part[3 * CH:4 * CH].astype(bf)

    @pl.when(j >= NB // 2)
    def _():
        pb[...] = part[CH:2 * CH].astype(bf)
        b2[...] = part[2 * CH:3 * CH].astype(bf)
        mb[...] = part[3 * CH:4 * CH]


def partial_counts(where, own, partner, tail, window, mine, peers, usable, e):
    anyspace = pl.BlockSpec(memory_space=pl.ANY)
    vmem = pl.BlockSpec(memory_space=pltpu.VMEM)
    jb = KD // NB
    low = pl.BlockSpec((CH, jb), lambda j: (0, jnp.minimum(j, NB // 2 - 1)))
    high = pl.BlockSpec((CH, jb), lambda j: (0, jnp.maximum(j - NB // 2, 0)))
    half = lambda t: jax.ShapeDtypeStruct((CH, HALF), t)
    bf, f32 = jnp.bfloat16, jnp.float32
    return pl.pallas_call(
        count_kernel,
        grid=(NB,),
        in_specs=[pl.BlockSpec(memory_space=pltpu.SMEM)] + [anyspace] * 3 + [vmem] * 4
        + [pl.BlockSpec((jb, FC), lambda j: (j, 0))],
        out_specs=[low, high, low, high, low, high, pl.BlockSpec((CH, jb), lambda j: (0, j))],
        out_shape=[half(bf), half(bf), half(f32), half(bf), half(bf), half(f32),
                   jax.ShapeDtypeStruct((CH, KD), f32)],
        scratch_shapes=[
            pltpu.VMEM((FE, D), bf),
            pltpu.VMEM((W, FC), bf),
            pltpu.SemaphoreType.DMA((3,)),
        ],
        name="counts",
    )(where, own, partner, tail, window, mine, peers, usable, e)


def along(block, axis, distance):
    n = lax.axis_size(axis)
    return lax.ppermute(block, axis, [(i, (i + distance) % n) for i in range(n)])


def segment_of(positions, starts):
    return jnp.sum((starts[None, :] <= positions[:, None]).astype(jnp.int32), axis=1)


def shards(frames, centers, starts):
    c = lax.axis_index("c")
    x = lax.axis_index("x")
    y = lax.axis_index("y")
    z = lax.axis_index("z")
    blocks = NZ * NX * NC
    partner = along(frames, "c", 1)
    last = frames[F - TAIL:]
    chips = ("z", "x", "c")
    tail = lax.ppermute(last, chips, [(i, i + 1) for i in range(1, blocks - 1, 2)])
    tail = tail + lax.ppermute(last, chips, [(i, i + 2) for i in range(1, blocks - 2, 2)])

    near = lax.dynamic_slice_in_dim(centers, c * (W // NC), W // NC, 0)
    given = jnp.where(y == 0, near, jnp.zeros_like(near))
    for d in range(1, NY):
        given = given + lax.ppermute(near, "y", [(0, d)])
    other = along(given, "c", 1)
    window = jnp.where(c == 0, jnp.concatenate([given, other]), jnp.concatenate([other, given]))
    window = window.reshape(NZ, NX, CH // NZ, D)

    first = (z * NX + x) * FC
    positions = first - TAIL + jnp.arange(FE, dtype=jnp.int32)
    usable = jnp.logical_and(
        segment_of(positions - LAG, starts) == segment_of(positions, starts), positions >= LAG
    ).astype(jnp.float32)[None, :] * (K * K / (blocks * F))

    where = jnp.stack([c, x]).astype(jnp.int32)
    e, mine, peers = memberships(where, frames, partner, tail, centers)
    peers = lax.all_to_all(peers, ("c", "y"), 0, 0, tiled=True)
    a2, b2, pa, pb, ma, mb, home = partial_counts(
        where, frames, partner, tail, window, mine, peers, usable, e
    )

    bf, f32 = jnp.bfloat16, jnp.float32
    via_a = along(a2, "x", 1)
    via_b = along(b2, "x", -1)
    up_b = along(pb, "x", 1)
    down_a = along(ma, "x", -1)
    up_a = along((pa + via_a.astype(f32)).astype(bf), "x", 1)
    down_b = along((mb + via_b.astype(f32)).astype(bf), "x", -1)
    low = home[:, :HALF] + up_a.astype(f32) + down_a.astype(f32)
    high = home[:, HALF:] + up_b.astype(f32) + down_b.astype(f32)
    gathered = jnp.concatenate([low, high], axis=1).reshape(NZ * NC, CH // (NZ * NC), KD)
    shares = lax.all_to_all(gathered.astype(SENT), ("z", "c"), 0, 0, tiled=True)
    summed = jnp.sum(shares.astype(f32).reshape(NZ, NC, CH // (NZ * NC), KD), axis=0)
    return jnp.concatenate([summed[0], summed[1]], axis=1)


SENT = jnp.float32


def solution(mesh):
    grid = Mesh(mesh.devices.reshape(NZ, NX, NC, NY), ("z", "x", "c", "y"))
    blocks = ("z", "x", "c")
    return jax.shard_map(
        shards,
        mesh=grid,
        in_specs=(P(blocks, None), P("y", None), P()),
        out_specs=P(blocks, "y"),
        check_vma=False,
    )
```

```python
import math

import jax
import jax.numpy as jnp
from jax import lax
from jax.experimental import pallas as pl
from jax.experimental.pallas import tpu as pltpu
from jax.sharding import Mesh, PartitionSpec as P

K = 16384
W = 512
LAG = 5
D = 512
SHARPNESS = 0.03125

NZ, NX, NC, NY = 8, 4, 2, 4
F = 1024
FC = NC * F
TAIL = 128
FE = TAIL + FC
KD = 2048
FB = 256
KB = 256
NB = FC // FB
CH = W // NX
HALF = KD // 2

LOG2E = math.log2(math.e)
DECAY = -SHARPNESS * LOG2E

SENT = jnp.float32


NT = (((1,), (1,)), ((), ()))
SMEM = pl.BlockSpec(memory_space=pltpu.SMEM)
VMEM = pl.BlockSpec(memory_space=pltpu.VMEM)
ANY = pl.BlockSpec(memory_space=pl.ANY)


def copy_all(pairs, sems):
    copies = [pltpu.make_async_copy(src, dst, sems.at[i]) for i, (src, dst) in enumerate(pairs)]
    for copy in copies:
        copy.start()
    for copy in copies:
        copy.wait()


def norm_kernel(where, centers, bias, cs, sems):
    copy_all([(centers.at[pl.ds(where[0] * KD, KD)], cs)], sems)

    def step(i, carry):
        at = pl.ds(pl.multiple_of(i * KB, KB), KB)
        block = cs[at, :].astype(jnp.float32)
        norm = jnp.sum(block * block, axis=1, keepdims=True)
        bias[at, :] = jnp.broadcast_to(norm, (KB, 128))
        return carry

    lax.fori_loop(0, KD // KB, step, 0)


def center_norms(where, centers):
    return pl.pallas_call(
        norm_kernel,
        in_specs=[SMEM, ANY],
        out_specs=VMEM,
        out_shape=jax.ShapeDtypeStruct((KD, 128), jnp.float32),
        scratch_shapes=[pltpu.VMEM((KD, D), jnp.bfloat16), pltpu.SemaphoreType.DMA((1,))],
        cost_estimate=pl.CostEstimate(flops=2 * KD * D, bytes_accessed=2 * KD * D, transcendentals=0),
        name="center_norms",
    )(where, centers)


def member_kernel(where, own, partner, tail, centers, norms, e_ref, st_ref, peers_ref,
                  xs, cs, bias, u0, u1, e0, e1, sems, out_sems):
    c = where[0]
    copy_all([
        (own, xs.at[pl.ds(TAIL + c * F, F)]),
        (partner, xs.at[pl.ds(TAIL + (1 - c) * F, F)]),
        (tail, xs.at[pl.ds(0, TAIL)]),
        (centers.at[pl.ds(c * KD, KD)], cs),
        (norms, bias),
    ], sems)
    slots = (u0, e0), (u1, e1)

    def out_copy(b, slot):
        start = pl.multiple_of(b * FB, FB)
        return pltpu.make_async_copy(slots[slot][1], e_ref.at[:, pl.ds(start, FB)], out_sems.at[slot])

    def stage(new, old):
        if new is not None:
            start, width, slot = new
            u = slots[slot][0]
            xb = xs[pl.ds(start, width), :]
            xf = xb.astype(jnp.float32)
            sq = xf * xf
            part = sq[:, 0:128] + sq[:, 128:256] + sq[:, 256:384] + sq[:, 384:512]
            frame = jnp.sum(part.T, axis=0, keepdims=True)
            twice = xb * jnp.bfloat16(-2.0)
            least = None
        if old is not None:
            start_o, width_o, slot_o, keep, least_o = old
            u_o, e_o = slots[slot_o]
            total = None
        for i in range(KD // KB):
            rows = slice(i * KB, (i + 1) * KB)
            if new is not None:
                ip = lax.dot_general(cs[rows, :], twice, NT, preferred_element_type=jnp.float32)
                b = bias[rows, :]
                v = (frame + ip) + (b if width == 128 else jnp.concatenate([b] * (width // 128), axis=1))
                u[rows, 0:width] = v
                h = jnp.min(v.reshape(KB // 8, 8, width), axis=0)
                least = h if least is None else jnp.minimum(least, h)
            if old is not None:
                e = jnp.exp2((u_o[rows, 0:width_o] - least_o) * DECAY)
                t = jnp.sum(e.reshape(KB // 8, 8, width_o), axis=0)
                total = t if total is None else total + t
                if keep:
                    e_o[rows, :] = e
        if old is not None:
            total = jnp.sum(total, axis=0, keepdims=True)
            both = jnp.concatenate([least_o, total], axis=0)
            peers_ref[:, :, pl.ds(start_o, width_o)] = jnp.broadcast_to(both[None], (NC * NY, 2, width_o))
        if new is not None:
            least = jnp.min(least, axis=0, keepdims=True)
            st_ref[0:1, pl.ds(start, width)] = least
            st_ref[1:2, pl.ds(start, width)] = frame
            return least

    def at(b):
        return pl.multiple_of(TAIL + b * FB, 128)

    least = stage((0, TAIL, 1), None)
    least = stage((TAIL, FB, 0), (0, TAIL, 1, False, least))

    def step(k, least):
        for half in range(2):
            b = 2 * k + half

            @pl.when(k > 0)
            def _():
                out_copy(b - 2, half).wait()

            least = stage((at(b + 1), FB, 1 - half), (at(b), FB, half, True, least))
            out_copy(b, half).start()
        return least

    least = lax.fori_loop(0, NB // 2 - 1, step, least)
    out_copy(NB - 4, 0).wait()
    least = stage((at(NB - 1), FB, 1), (at(NB - 2), FB, 0, True, least))
    out_copy(NB - 2, 0).start()
    out_copy(NB - 3, 1).wait()
    stage(None, (at(NB - 1), FB, 1, True, least))
    out_copy(NB - 1, 1).start()
    out_copy(NB - 2, 0).wait()
    out_copy(NB - 1, 1).wait()


def memberships(where, own, partner, tail, centers, norms):
    return pl.pallas_call(
        member_kernel,
        in_specs=[SMEM] + [ANY] * 5,
        out_specs=[ANY, VMEM, VMEM],
        out_shape=[
            jax.ShapeDtypeStruct((KD, FC), jnp.float32),
            jax.ShapeDtypeStruct((2, FE), jnp.float32),
            jax.ShapeDtypeStruct((NC * NY, 2, FE), jnp.float32),
        ],
        scratch_shapes=[
            pltpu.VMEM((FE, D), jnp.bfloat16),
            pltpu.VMEM((KD, D), jnp.bfloat16),
            pltpu.VMEM((KD, 128), jnp.float32),
            pltpu.VMEM((KD, FB), jnp.float32),
            pltpu.VMEM((KD, FB), jnp.float32),
            pltpu.VMEM((KD, FB), jnp.float32),
            pltpu.VMEM((KD, FB), jnp.float32),
            pltpu.SemaphoreType.DMA((5,)),
            pltpu.SemaphoreType.DMA((2,)),
        ],
        cost_estimate=pl.CostEstimate(flops=2 * KD * FE * D, bytes_accessed=2 * (KD * FC + KD * D + FE * D),
                                      transcendentals=KD * FE),
        name="memberships",
    )(where, own, partner, tail, centers, norms)


def window_kernel(where, own, partner, tail, window, mine, out):
    c = where[0]
    x = where[1]
    z = where[2]
    parts = ((tail, 0, TAIL), (own, TAIL + c * F, F), (partner, TAIL + (1 - c) * F, F))
    twice = [ref[...] * jnp.bfloat16(-2.0) for ref, _, _ in parts]
    for d in range(NX):
        rows = jnp.concatenate([window[lax.rem(z + s, NZ), lax.rem(x + d, NX)] for s in range(NZ)], axis=0)
        rf = rows.astype(jnp.float32)
        norm = jnp.sum(rf * rf, axis=1, keepdims=True)
        for (_, start, width), xb in zip(parts, twice):
            at = pl.ds(pl.multiple_of(start, 128), width)
            ip = lax.dot_general(rows, xb, NT, preferred_element_type=jnp.float32)
            out[d * CH:(d + 1) * CH, at] = (mine[1:2, at] + ip) + norm


def window_distances(where, own, partner, tail, window, mine):
    return pl.pallas_call(
        window_kernel,
        in_specs=[SMEM] + [VMEM] * 5,
        out_specs=VMEM,
        out_shape=jax.ShapeDtypeStruct((W, FE), jnp.float32),
        cost_estimate=pl.CostEstimate(flops=2 * W * FE * D, bytes_accessed=4 * W * FE, transcendentals=0),
        name="window_distances",
    )(where, own, partner, tail, window, mine)


def count_kernel(distances, mine, peers, usable, e_ref, a2, b2, pa, pb, ma, mb, home, lead, factor):
    j = pl.program_id(0)

    @pl.when(j == 0)
    def _():
        mins = peers[:, 0, :]
        least = jnp.min(mins, axis=0, keepdims=True)
        total = jnp.sum(peers[:, 1, :] * jnp.exp2((mins - least) * DECAY), axis=0, keepdims=True)
        inverse = 1.0 / total
        lag_scale = jnp.exp2((mine[0:1, :] - least) * DECAY) * inverse
        factor[...] = lag_scale[:, TAIL:]
        scale = inverse * pltpu.roll(usable[...], FE - LAG, 1)
        for r in range(0, W, 64):
            m = jnp.exp2((distances[r:r + 64, :] - least) * DECAY) * scale
            lead[r:r + 64, :] = pltpu.roll(m, LAG, 1)[:, TAIL:].astype(jnp.bfloat16)

    member = (e_ref[...] * factor[...]).astype(jnp.bfloat16)
    part = lax.dot_general(lead[...], member, NT, preferred_element_type=jnp.float32)
    home[...] = part[0:CH]

    @pl.when(j < NB // 2)
    def _():
        pa[...] = part[CH:2 * CH].astype(pa.dtype)
        a2[...] = part[2 * CH:3 * CH].astype(a2.dtype)
        ma[...] = part[3 * CH:4 * CH].astype(ma.dtype)

    @pl.when(j >= NB // 2)
    def _():
        pb[...] = part[CH:2 * CH].astype(pb.dtype)
        b2[...] = part[2 * CH:3 * CH].astype(b2.dtype)
        mb[...] = part[3 * CH:4 * CH].astype(mb.dtype)


def partial_counts(distances, mine, peers, usable, e):
    jb = KD // NB
    low = pl.BlockSpec((CH, jb), lambda j: (0, jnp.minimum(j, NB // 2 - 1)))
    high = pl.BlockSpec((CH, jb), lambda j: (0, jnp.maximum(j - NB // 2, 0)))
    half = lambda t: jax.ShapeDtypeStruct((CH, HALF), t)
    f32 = jnp.float32
    return pl.pallas_call(
        count_kernel,
        grid=(NB,),
        in_specs=[VMEM] * 4 + [pl.BlockSpec((jb, FC), lambda j: (j, 0))],
        out_specs=[low, high, low, high, low, high, pl.BlockSpec((CH, jb), lambda j: (0, j))],
        out_shape=[half(SENT), half(SENT), half(f32), half(SENT), half(SENT), half(f32),
                   jax.ShapeDtypeStruct((CH, KD), f32)],
        scratch_shapes=[pltpu.VMEM((W, FC), jnp.bfloat16), pltpu.VMEM((1, FC), f32)],
        cost_estimate=pl.CostEstimate(flops=2 * W * FC * KD, bytes_accessed=4 * FC * KD + 4 * W * FE,
                                      transcendentals=W * FE),
        name="counts",
    )(distances, mine, peers, usable, e)


def along(block, axis, distance):
    n = lax.axis_size(axis)
    return lax.ppermute(block, axis, [(i, (i + distance) % n) for i in range(n)])


def segment_of(positions, starts):
    return jnp.sum((starts[None, :] <= positions[:, None]).astype(jnp.int32), axis=1)


def shards(frames, centers, starts):
    c = lax.axis_index("c")
    x = lax.axis_index("x")
    y = lax.axis_index("y")
    z = lax.axis_index("z")
    blocks = NZ * NX * NC
    partner = along(frames, "c", 1)
    last = frames[F - TAIL:]
    chips = ("z", "x", "c")
    tail = lax.ppermute(last, chips, [(i, i + 1) for i in range(1, blocks - 1, 2)])
    tail = tail + lax.ppermute(last, chips, [(i, i + 2) for i in range(1, blocks - 2, 2)])

    near = lax.dynamic_slice_in_dim(centers, c * (W // NC), W // NC, 0)
    sent = [lax.ppermute(near, "y", [(0, d)]) for d in range(1, NY)]

    first = (z * NX + x) * FC
    positions = first - TAIL + jnp.arange(FE, dtype=jnp.int32)
    usable = jnp.logical_and(
        segment_of(positions - LAG, starts) == segment_of(positions, starts), positions >= LAG
    ).astype(jnp.float32)[None, :] * (K * K / (blocks * F))

    where = jnp.stack([c, x, z]).astype(jnp.int32)
    norms = center_norms(where, centers)
    e, mine, peers = memberships(where, frames, partner, tail, centers, norms)
    given = jnp.where(y == 0, near, jnp.zeros_like(near))
    sent, e = lax.optimization_barrier((sent, e))
    for part in sent:
        given = given + part
    other = along(given, "c", 1)
    peers, given = lax.optimization_barrier((peers, given))
    peers = lax.all_to_all(peers, ("c", "y"), 0, 0, tiled=True)
    window = jnp.where(c == 0, jnp.concatenate([given, other]), jnp.concatenate([other, given]))
    window = window.reshape(NZ, NX, CH // NZ, D)
    distances = window_distances(where, frames, partner, tail, window, mine)
    a2, b2, pa, pb, ma, mb, home = partial_counts(distances, mine, peers, usable, e)

    f32 = jnp.float32
    via_a = along(a2, "x", 1)
    via_b = along(b2, "x", -1)
    up_b = along(pb, "x", 1)
    down_a = along(ma, "x", -1)
    up_a = along((pa + via_a.astype(f32)).astype(SENT), "x", 1)
    down_b = along((mb + via_b.astype(f32)).astype(SENT), "x", -1)
    low = home[:, :HALF] + up_a.astype(f32) + down_a.astype(f32)
    high = home[:, HALF:] + up_b.astype(f32) + down_b.astype(f32)
    share = jnp.concatenate([low, high], axis=1).reshape(NZ, CH // NZ, KD)
    far_up = along(share[4, :, :HALF], "z", 2)
    far_down = along(share[4, :, HALF:], "z", -2)
    up = along(share[3], "z", 1)
    down = along(share[5], "z", -1)
    up = along(share[2] + up + jnp.pad(far_up, ((0, 0), (0, HALF))), "z", 1)
    down = along(share[6] + down + jnp.pad(far_down, ((0, 0), (HALF, 0))), "z", -1)
    up = along(share[1] + up, "z", 1)
    down = along(share[7] + down, "z", -1)
    summed = (share[0] + up + down).reshape(NC, CH // (NZ * NC), KD)
    mine = jnp.where(c == 0, summed[0], summed[1])
    other = along(jnp.where(c == 0, summed[1], summed[0]), "c", 1)
    return jnp.where(c == 0, jnp.concatenate([mine, other], axis=1), jnp.concatenate([other, mine], axis=1))


def solution(mesh):
    grid = Mesh(mesh.devices.reshape(NZ, NX, NC, NY), ("z", "x", "c", "y"))
    blocks = ("z", "x", "c")
    return jax.shard_map(
        shards,
        mesh=grid,
        in_specs=(P(blocks, None), P("y", None), P()),
        out_specs=P(blocks, "y"),
        check_vma=False,
    )
```

```python
import math

import jax
import jax.numpy as jnp
from jax import lax
from jax.experimental import pallas as pl
from jax.experimental.pallas import tpu as pltpu
from jax.sharding import Mesh, PartitionSpec as P

K = 16384
W = 512
LAG = 5
D = 512
SHARPNESS = 0.03125

NZ, NX, NC, NY = 8, 4, 2, 4
F = 1024
FC = NC * F
TAIL = 128
FE = TAIL + FC
KD = 2048
FB = 256
KB = 256
NB = FC // FB
CH = W // NX
HALF = KD // 2

LOG2E = math.log2(math.e)
DECAY = -SHARPNESS * LOG2E

SENT = jnp.float16


NT = (((1,), (1,)), ((), ()))
SMEM = pl.BlockSpec(memory_space=pltpu.SMEM)
VMEM = pl.BlockSpec(memory_space=pltpu.VMEM)
ANY = pl.BlockSpec(memory_space=pl.ANY)


def copy_all(pairs, sems):
    copies = [pltpu.make_async_copy(src, dst, sems.at[i]) for i, (src, dst) in enumerate(pairs)]
    for copy in copies:
        copy.start()
    for copy in copies:
        copy.wait()


def member_kernel(where, own, partner, tail, centers, e_ref, st_ref, peers_ref,
                  xs, cs, bias, u0, u1, e0, e1, sems, out_sems):
    c = where[0]
    copy_all([
        (own, xs.at[pl.ds(TAIL + c * F, F)]),
        (partner, xs.at[pl.ds(TAIL + (1 - c) * F, F)]),
        (tail, xs.at[pl.ds(0, TAIL)]),
        (centers.at[pl.ds(c * KD, KD)], cs),
    ], sems)
    for i in range(KD // KB):
        block = cs[i * KB:(i + 1) * KB, :].astype(jnp.float32)
        norm = jnp.sum(block * block, axis=1, keepdims=True)
        bias[i * KB:(i + 1) * KB, :] = jnp.broadcast_to(norm, (KB, 128))
    slots = (u0, e0), (u1, e1)

    def out_copy(b, slot):
        start = pl.multiple_of(b * FB, FB)
        return pltpu.make_async_copy(slots[slot][1], e_ref.at[:, pl.ds(start, FB)], out_sems.at[slot])

    def stage(new, old):
        if new is not None:
            start, width, slot = new
            u = slots[slot][0]
            xb = xs[pl.ds(start, width), :]
            xf = xb.astype(jnp.float32)
            sq = xf * xf
            part = sq[:, 0:128] + sq[:, 128:256] + sq[:, 256:384] + sq[:, 384:512]
            frame = jnp.sum(part.T, axis=0, keepdims=True)
            twice = xb * jnp.bfloat16(-2.0)
            least = None
        if old is not None:
            start_o, width_o, slot_o, keep, least_o = old
            u_o, e_o = slots[slot_o]
            total = None
        for i in range(KD // KB):
            rows = slice(i * KB, (i + 1) * KB)
            if new is not None:
                ip = lax.dot_general(cs[rows, :], twice, NT, preferred_element_type=jnp.float32)
                b = bias[rows, :]
                v = (frame + ip) + (b if width == 128 else jnp.concatenate([b] * (width // 128), axis=1))
                u[rows, 0:width] = v
                h = jnp.min(v.reshape(KB // 8, 8, width), axis=0)
                least = h if least is None else jnp.minimum(least, h)
            if old is not None:
                e = jnp.exp2((u_o[rows, 0:width_o] - least_o) * DECAY)
                t = jnp.sum(e.reshape(KB // 8, 8, width_o), axis=0)
                total = t if total is None else total + t
                if keep:
                    e_o[rows, :] = e
        if old is not None:
            total = jnp.sum(total, axis=0, keepdims=True)
            both = jnp.concatenate([least_o, total], axis=0)
            peers_ref[:, :, pl.ds(start_o, width_o)] = jnp.broadcast_to(both[None], (NC * NY, 2, width_o))
        if new is not None:
            least = jnp.min(least, axis=0, keepdims=True)
            st_ref[0:1, pl.ds(start, width)] = least
            st_ref[1:2, pl.ds(start, width)] = frame
            return least

    def at(b):
        return pl.multiple_of(TAIL + b * FB, 128)

    least = stage((0, TAIL, 1), None)
    least = stage((TAIL, FB, 0), (0, TAIL, 1, False, least))

    def step(k, least):
        for half in range(2):
            b = 2 * k + half

            @pl.when(k > 0)
            def _():
                out_copy(b - 2, half).wait()

            least = stage((at(b + 1), FB, 1 - half), (at(b), FB, half, True, least))
            out_copy(b, half).start()
        return least

    least = lax.fori_loop(0, NB // 2 - 1, step, least)
    out_copy(NB - 4, 0).wait()
    least = stage((at(NB - 1), FB, 1), (at(NB - 2), FB, 0, True, least))
    out_copy(NB - 2, 0).start()
    out_copy(NB - 3, 1).wait()
    stage(None, (at(NB - 1), FB, 1, True, least))
    out_copy(NB - 1, 1).start()
    out_copy(NB - 2, 0).wait()
    out_copy(NB - 1, 1).wait()


def memberships(where, own, partner, tail, centers):
    return pl.pallas_call(
        member_kernel,
        in_specs=[SMEM] + [ANY] * 4,
        out_specs=[ANY, VMEM, VMEM],
        out_shape=[
            jax.ShapeDtypeStruct((KD, FC), jnp.float32),
            jax.ShapeDtypeStruct((2, FE), jnp.float32),
            jax.ShapeDtypeStruct((NC * NY, 2, FE), jnp.float32),
        ],
        scratch_shapes=[
            pltpu.VMEM((FE, D), jnp.bfloat16),
            pltpu.VMEM((KD, D), jnp.bfloat16),
            pltpu.VMEM((KD, 128), jnp.float32),
            pltpu.VMEM((KD, FB), jnp.float32),
            pltpu.VMEM((KD, FB), jnp.float32),
            pltpu.VMEM((KD, FB), jnp.float32),
            pltpu.VMEM((KD, FB), jnp.float32),
            pltpu.SemaphoreType.DMA((4,)),
            pltpu.SemaphoreType.DMA((2,)),
        ],
        cost_estimate=pl.CostEstimate(flops=2 * KD * FE * D, bytes_accessed=2 * (KD * FC + KD * D + FE * D),
                                      transcendentals=KD * FE),
        name="memberships",
    )(where, own, partner, tail, centers)


def window_kernel(where, own, partner, tail, window, mine, out):
    c = where[0]
    x = where[1]
    parts = ((tail, 0, TAIL), (own, TAIL + c * F, F), (partner, TAIL + (1 - c) * F, F))
    twice = [ref[...] * jnp.bfloat16(-2.0) for ref, _, _ in parts]
    for d in range(NX):
        rows = jnp.concatenate([window[s, lax.rem(x + d, NX)] for s in range(NZ)], axis=0)
        rf = rows.astype(jnp.float32)
        norm = jnp.sum(rf * rf, axis=1, keepdims=True)
        for (_, start, width), xb in zip(parts, twice):
            at = pl.ds(pl.multiple_of(start, 128), width)
            ip = lax.dot_general(rows, xb, NT, preferred_element_type=jnp.float32)
            out[d * CH:(d + 1) * CH, at] = (mine[1:2, at] + ip) + norm


def window_distances(where, own, partner, tail, window, mine):
    return pl.pallas_call(
        window_kernel,
        in_specs=[SMEM] + [VMEM] * 5,
        out_specs=VMEM,
        out_shape=jax.ShapeDtypeStruct((W, FE), jnp.float32),
        cost_estimate=pl.CostEstimate(flops=2 * W * FE * D, bytes_accessed=4 * W * FE, transcendentals=0),
        name="window_distances",
    )(where, own, partner, tail, window, mine)


def count_kernel(distances, mine, peers, usable, e_ref, a2, b2, pa, pb, ma, mb, home, level, lead, factor, largest):
    j = pl.program_id(0)

    @pl.when(j == 0)
    def _():
        mins = peers[:, 0, :]
        least = jnp.min(mins, axis=0, keepdims=True)
        total = jnp.sum(peers[:, 1, :] * jnp.exp2((mins - least) * DECAY), axis=0, keepdims=True)
        inverse = 1.0 / total
        lag_scale = jnp.exp2((mine[0:1, :] - least) * DECAY) * inverse
        factor[...] = lag_scale[:, TAIL:]
        scale = inverse * pltpu.roll(usable[...], FE - LAG, 1)
        for r in range(0, W, 64):
            m = jnp.exp2((distances[r:r + 64, :] - least) * DECAY) * scale
            lead[r:r + 64, :] = pltpu.roll(m, LAG, 1)[:, TAIL:].astype(jnp.bfloat16)

    member = (e_ref[...] * factor[...]).astype(jnp.bfloat16)
    part = lax.dot_general(lead[...], member, NT, preferred_element_type=jnp.float32)
    home[...] = part[0:CH]
    height = jnp.max(part.reshape(W // 8, 8, FB), axis=0)
    height = jnp.maximum(height[:, 0:128], height[:, 128:256])
    largest[...] = jnp.where(j == 0, height, jnp.maximum(largest[...], height))

    @pl.when(j == NB - 1)
    def _():
        most = jnp.max(jnp.max(largest[...], axis=1, keepdims=True), axis=0, keepdims=True)
        level[...] = jnp.broadcast_to(jnp.ceil(jnp.log2(jnp.maximum(most, 1e-30))) - 14.0, (8, 128))

    @pl.when(j < NB // 2)
    def _():
        pa[...] = part[CH:2 * CH]
        a2[...] = part[2 * CH:3 * CH]
        ma[...] = part[3 * CH:4 * CH]

    @pl.when(j >= NB // 2)
    def _():
        pb[...] = part[CH:2 * CH]
        b2[...] = part[2 * CH:3 * CH]
        mb[...] = part[3 * CH:4 * CH]


def partial_counts(distances, mine, peers, usable, e):
    jb = KD // NB
    low = pl.BlockSpec((CH, jb), lambda j: (0, jnp.minimum(j, NB // 2 - 1)))
    high = pl.BlockSpec((CH, jb), lambda j: (0, jnp.maximum(j - NB // 2, 0)))
    f32 = jnp.float32
    half = jax.ShapeDtypeStruct((CH, HALF), f32)
    return pl.pallas_call(
        count_kernel,
        grid=(NB,),
        in_specs=[VMEM] * 4 + [pl.BlockSpec((jb, FC), lambda j: (j, 0))],
        out_specs=[low, high, low, high, low, high, pl.BlockSpec((CH, jb), lambda j: (0, j)),
                   pl.BlockSpec((8, 128), lambda j: (0, 0))],
        out_shape=[half] * 6 + [jax.ShapeDtypeStruct((CH, KD), f32), jax.ShapeDtypeStruct((8, 128), f32)],
        scratch_shapes=[pltpu.VMEM((W, FC), jnp.bfloat16), pltpu.VMEM((1, FC), f32), pltpu.VMEM((8, 128), f32)],
        cost_estimate=pl.CostEstimate(flops=2 * W * FC * KD, bytes_accessed=4 * FC * KD + 4 * W * FE,
                                      transcendentals=W * FE),
        name="counts",
    )(distances, mine, peers, usable, e)


def along(block, axis, distance):
    n = lax.axis_size(axis)
    return lax.ppermute(block, axis, [(i, (i + distance) % n) for i in range(n)])


def packed(counts, level):
    note = jnp.broadcast_to(level.astype(SENT), (8, counts.shape[1]))
    return jnp.concatenate([(counts * jnp.exp2(-level)).astype(SENT), note], axis=0)


def level_of(message):
    return message[-1:, 0:1].astype(jnp.float32)


def opened(message):
    return message[:-8].astype(jnp.float32) * jnp.exp2(level_of(message))


def segment_of(positions, starts):
    return jnp.sum((starts[None, :] <= positions[:, None]).astype(jnp.int32), axis=1)


def shards(frames, centers, starts):
    c = lax.axis_index("c")
    x = lax.axis_index("x")
    y = lax.axis_index("y")
    z = lax.axis_index("z")
    blocks = NZ * NX * NC
    partner = along(frames, "c", 1)
    last = frames[F - TAIL:]
    chips = ("z", "x", "c")
    tail = lax.ppermute(last, chips, [(i, i + 1) for i in range(1, blocks - 1, 2)])
    tail = tail + lax.ppermute(last, chips, [(i, i + 2) for i in range(1, blocks - 2, 2)])

    near = lax.dynamic_slice_in_dim(centers, c * (W // NC), W // NC, 0)
    sent = [lax.ppermute(near, "y", [(0, d)]) for d in range(1, NY)]

    first = (z * NX + x) * FC
    positions = first - TAIL + jnp.arange(FE, dtype=jnp.int32)
    usable = jnp.logical_and(
        segment_of(positions - LAG, starts) == segment_of(positions, starts), positions >= LAG
    ).astype(jnp.float32)[None, :] * (K * K / (blocks * F))

    where = jnp.stack([c, x]).astype(jnp.int32)
    e, mine, peers = memberships(where, frames, partner, tail, centers)
    given = jnp.where(y == 0, near, jnp.zeros_like(near))
    sent, e = lax.optimization_barrier((sent, e))
    for part in sent:
        given = given + part
    other = along(given, "c", 1)
    peers, given = lax.optimization_barrier((peers, given))
    peers = lax.all_to_all(peers, ("c", "y"), 0, 0, tiled=True)
    window = jnp.where(c == 0, jnp.concatenate([given, other]), jnp.concatenate([other, given]))
    window = window.reshape(NZ, NX, CH // NZ, D)
    distances = window_distances(where, frames, partner, tail, window, mine)
    a2, b2, pa, pb, ma, mb, home, level = partial_counts(distances, mine, peers, usable, e)

    level = level[0:1, 0:1]
    via_a = along(packed(a2, level), "x", 1)
    via_b = along(packed(b2, level), "x", -1)
    up_b = along(packed(pb, level), "x", 1)
    down_a = along(packed(ma, level), "x", -1)
    raised = jnp.maximum(level, level_of(via_a)) + 1.0
    up_a = along(packed(pa + opened(via_a), raised), "x", 1)
    raised = jnp.maximum(level, level_of(via_b)) + 1.0
    down_b = along(packed(mb + opened(via_b), raised), "x", -1)
    low = home[:, :HALF] + opened(up_a) + opened(down_a)
    high = home[:, HALF:] + opened(up_b) + opened(down_b)
    for part in (up_a, up_b, down_a, down_b):
        level = jnp.maximum(level, level_of(part))
    level = level + 2.0
    rows = CH // (NZ * NC)
    share = (jnp.concatenate([low, high], axis=1) * jnp.exp2(-level)).astype(SENT).reshape(NZ * NC, rows, KD)
    note = jnp.broadcast_to(level.astype(SENT), (NZ * NC, rows, 128))
    shares = lax.all_to_all(jnp.concatenate([share, note], axis=2), ("z", "c"), 0, 0, tiled=True)
    shares = shares.astype(jnp.float32)
    shares = shares[:, :, :KD] * jnp.exp2(shares[:, :, KD:KD + 1])
    summed = jnp.sum(shares.reshape(NZ, NC, rows, KD), axis=0)
    return jnp.concatenate([summed[0], summed[1]], axis=1)


def solution(mesh):
    grid = Mesh(mesh.devices.reshape(NZ, NX, NC, NY), ("z", "x", "c", "y"))
    blocks = ("z", "x", "c")
    return jax.shard_map(
        shards,
        mesh=grid,
        in_specs=(P(blocks, None), P("y", None), P()),
        out_specs=P(blocks, "y"),
        check_vma=False,
    )
```

```python
import math

import jax
import jax.numpy as jnp
from jax import lax
from jax.experimental import pallas as pl
from jax.experimental.pallas import tpu as pltpu
from jax.sharding import Mesh, PartitionSpec as P

K = 16384
W = 512
LAG = 5
D = 512
SHARPNESS = 0.03125

NZ, NX, NC, NY = 8, 4, 2, 4
F = 1024
FC = NC * F
TAIL = 128
FE = TAIL + FC
KD = 2048
FB = 256
KB = 256
NB = FC // FB
CH = W // NX
HALF = KD // 2

LOG2E = math.log2(math.e)
DECAY = -SHARPNESS * LOG2E

SENT = jnp.float16
ROOT_SCALE = 8.0


NT = (((1,), (1,)), ((), ()))
SMEM = pl.BlockSpec(memory_space=pltpu.SMEM)
VMEM = pl.BlockSpec(memory_space=pltpu.VMEM)
ANY = pl.BlockSpec(memory_space=pl.ANY)


def copy_all(pairs, sems):
    copies = [pltpu.make_async_copy(src, dst, sems.at[i]) for i, (src, dst) in enumerate(pairs)]
    for copy in copies:
        copy.start()
    for copy in copies:
        copy.wait()


def member_kernel(where, own, partner, tail, centers, e_ref, st_ref, peers_ref,
                  xs, cs, bias, u0, u1, e0, e1, sems, out_sems):
    c = where[0]
    copy_all([
        (own, xs.at[pl.ds(TAIL + c * F, F)]),
        (partner, xs.at[pl.ds(TAIL + (1 - c) * F, F)]),
        (tail, xs.at[pl.ds(0, TAIL)]),
        (centers.at[pl.ds(c * KD, KD)], cs),
    ], sems)
    for i in range(KD // KB):
        block = cs[i * KB:(i + 1) * KB, :].astype(jnp.float32)
        norm = jnp.sum(block * block, axis=1, keepdims=True)
        bias[i * KB:(i + 1) * KB, :] = jnp.broadcast_to(norm, (KB, 128))
    slots = (u0, e0), (u1, e1)

    def out_copy(b, slot):
        start = pl.multiple_of(b * FB, FB)
        return pltpu.make_async_copy(slots[slot][1], e_ref.at[:, pl.ds(start, FB)], out_sems.at[slot])

    def stage(new, old):
        if new is not None:
            start, width, slot = new
            u = slots[slot][0]
            xb = xs[pl.ds(start, width), :]
            xf = xb.astype(jnp.float32)
            sq = xf * xf
            part = sq[:, 0:128] + sq[:, 128:256] + sq[:, 256:384] + sq[:, 384:512]
            frame = jnp.sum(part.T, axis=0, keepdims=True)
            twice = xb * jnp.bfloat16(-2.0)
            least = None
        if old is not None:
            start_o, width_o, slot_o, keep, least_o = old
            u_o, e_o = slots[slot_o]
            total = None
        for i in range(KD // KB):
            rows = slice(i * KB, (i + 1) * KB)
            if new is not None:
                ip = lax.dot_general(cs[rows, :], twice, NT, preferred_element_type=jnp.float32)
                b = bias[rows, :]
                v = (frame + ip) + (b if width == 128 else jnp.concatenate([b] * (width // 128), axis=1))
                u[rows, 0:width] = v
                h = jnp.min(v.reshape(KB // 8, 8, width), axis=0)
                least = h if least is None else jnp.minimum(least, h)
            if old is not None:
                e = jnp.exp2((u_o[rows, 0:width_o] - least_o) * DECAY)
                t = jnp.sum(e.reshape(KB // 8, 8, width_o), axis=0)
                total = t if total is None else total + t
                if keep:
                    e_o[rows, :] = e
        if old is not None:
            total = jnp.sum(total, axis=0, keepdims=True)
            both = jnp.concatenate([least_o, total], axis=0)
            peers_ref[:, :, pl.ds(start_o, width_o)] = jnp.broadcast_to(both[None], (NC * NY, 2, width_o))
        if new is not None:
            least = jnp.min(least, axis=0, keepdims=True)
            st_ref[0:1, pl.ds(start, width)] = least
            st_ref[1:2, pl.ds(start, width)] = frame
            return least

    def at(b):
        return pl.multiple_of(TAIL + b * FB, 128)

    least = stage((0, TAIL, 1), None)
    least = stage((TAIL, FB, 0), (0, TAIL, 1, False, least))

    def step(k, least):
        for half in range(2):
            b = 2 * k + half

            @pl.when(k > 0)
            def _():
                out_copy(b - 2, half).wait()

            least = stage((at(b + 1), FB, 1 - half), (at(b), FB, half, True, least))
            out_copy(b, half).start()
        return least

    least = lax.fori_loop(0, NB // 2 - 1, step, least)
    out_copy(NB - 4, 0).wait()
    least = stage((at(NB - 1), FB, 1), (at(NB - 2), FB, 0, True, least))
    out_copy(NB - 2, 0).start()
    out_copy(NB - 3, 1).wait()
    stage(None, (at(NB - 1), FB, 1, True, least))
    out_copy(NB - 1, 1).start()
    out_copy(NB - 2, 0).wait()
    out_copy(NB - 1, 1).wait()


def memberships(where, own, partner, tail, centers):
    return pl.pallas_call(
        member_kernel,
        in_specs=[SMEM] + [ANY] * 4,
        out_specs=[ANY, VMEM, VMEM],
        out_shape=[
            jax.ShapeDtypeStruct((KD, FC), jnp.float32),
            jax.ShapeDtypeStruct((2, FE), jnp.float32),
            jax.ShapeDtypeStruct((NC * NY, 2, FE), jnp.float32),
        ],
        scratch_shapes=[
            pltpu.VMEM((FE, D), jnp.bfloat16),
            pltpu.VMEM((KD, D), jnp.bfloat16),
            pltpu.VMEM((KD, 128), jnp.float32),
            pltpu.VMEM((KD, FB), jnp.float32),
            pltpu.VMEM((KD, FB), jnp.float32),
            pltpu.VMEM((KD, FB), jnp.float32),
            pltpu.VMEM((KD, FB), jnp.float32),
            pltpu.SemaphoreType.DMA((4,)),
            pltpu.SemaphoreType.DMA((2,)),
        ],
        cost_estimate=pl.CostEstimate(flops=2 * KD * FE * D, bytes_accessed=2 * (KD * FC + KD * D + FE * D),
                                      transcendentals=KD * FE),
        name="memberships",
    )(where, own, partner, tail, centers)


def window_kernel(where, own, partner, tail, window, mine, out, twice):
    c = where[0]
    d = pl.program_id(0)

    @pl.when(d == 0)
    def _():
        for ref, start in ((tail, 0), (own, TAIL + c * F), (partner, TAIL + (1 - c) * F)):
            twice[pl.ds(pl.multiple_of(start, 128), ref.shape[0]), :] = ref[...] * jnp.bfloat16(-2.0)

    turn = lax.rem(where[1] + d, NX)
    rows = jnp.concatenate([window[s, turn] for s in range(NZ)], axis=0)
    rf = rows.astype(jnp.float32)
    norm = jnp.sum(rf * rf, axis=1, keepdims=True)
    ip = lax.dot_general(rows, twice[...], NT, preferred_element_type=jnp.float32)
    out[...] = (mine[1:2, :] + ip) + norm


def window_distances(where, own, partner, tail, window, mine):
    return pl.pallas_call(
        window_kernel,
        grid=(NX,),
        in_specs=[SMEM] + [VMEM] * 5,
        out_specs=pl.BlockSpec((CH, FE), lambda d: (d, 0)),
        out_shape=jax.ShapeDtypeStruct((W, FE), jnp.float32),
        scratch_shapes=[pltpu.VMEM((FE, D), jnp.bfloat16)],
        cost_estimate=pl.CostEstimate(flops=2 * W * FE * D, bytes_accessed=4 * W * FE, transcendentals=0),
        name="window_distances",
    )(where, own, partner, tail, window, mine)


def count_kernel(distances, mine, peers, usable, e_ref, a2, b2, pa, pb, ma, mb, home, lead, factor, level):
    step = pl.program_id(0)
    j = step - NX

    @pl.when(step == 0)
    def _():
        mins = peers[:, 0, :]
        least = jnp.min(mins, axis=0, keepdims=True)
        total = jnp.sum(peers[:, 1, :] * jnp.exp2((mins - least) * DECAY), axis=0, keepdims=True)
        inverse = 1.0 / total
        lag_scale = jnp.exp2((mine[0:1, :] - least) * DECAY) * inverse
        factor[...] = lag_scale[:, TAIL:]
        level[0:1, :] = least
        level[1:2, :] = inverse * pltpu.roll(usable[...], FE - LAG, 1)

    @pl.when(step < NX)
    def _():
        for r in range(0, CH, 64):
            m = jnp.exp2((distances[r:r + 64, :] - level[0:1, :]) * DECAY) * level[1:2, :]
            at = pl.ds(pl.multiple_of(step * CH + r, 64), 64)
            lead[at, :] = pltpu.roll(m, LAG, 1)[:, TAIL:].astype(jnp.bfloat16)

    def part_of():
        member = (e_ref[...] * factor[...]).astype(jnp.bfloat16)
        part = lax.dot_general(lead[...], member, NT, preferred_element_type=jnp.float32)
        home[...] = part[0:CH]
        return part[CH:2 * CH], part[2 * CH:3 * CH], part[3 * CH:4 * CH]

    @pl.when(jnp.logical_and(j >= 0, j < NB // 2))
    def _():
        pa[...], a2[...], ma[...] = part_of()

    @pl.when(j >= NB // 2)
    def _():
        pb[...], b2[...], mb[...] = part_of()


def partial_counts(distances, mine, peers, usable, e):
    jb = KD // NB
    low = pl.BlockSpec((CH, jb), lambda s: (0, jnp.clip(s - NX, 0, NB // 2 - 1)))
    high = pl.BlockSpec((CH, jb), lambda s: (0, jnp.maximum(s - NX - NB // 2, 0)))
    f32 = jnp.float32
    half = jax.ShapeDtypeStruct((CH, HALF), f32)
    return pl.pallas_call(
        count_kernel,
        grid=(NX + NB,),
        in_specs=[pl.BlockSpec((CH, FE), lambda s: (jnp.minimum(s, NX - 1), 0))] + [VMEM] * 3
        + [pl.BlockSpec((jb, FC), lambda s: (jnp.maximum(s - NX, 0), 0))],
        out_specs=[low, high, low, high, low, high, pl.BlockSpec((CH, jb), lambda s: (0, jnp.maximum(s - NX, 0)))],
        out_shape=[half] * 6 + [jax.ShapeDtypeStruct((CH, KD), f32)],
        scratch_shapes=[pltpu.VMEM((W, FC), jnp.bfloat16), pltpu.VMEM((1, FC), f32), pltpu.VMEM((2, FE), f32)],
        cost_estimate=pl.CostEstimate(flops=2 * W * FC * KD, bytes_accessed=4 * FC * KD + 4 * W * FE,
                                      transcendentals=W * FE),
        name="counts",
    )(distances, mine, peers, usable, e)


def along(block, axis, distance):
    n = lax.axis_size(axis)
    return lax.ppermute(block, axis, [(i, (i + distance) % n) for i in range(n)])


def packed(counts):
    return (jnp.sqrt(counts) * ROOT_SCALE).astype(SENT)


def opened(message):
    root = message.astype(jnp.float32) * (1.0 / ROOT_SCALE)
    return root * root


def segment_of(positions, starts):
    return jnp.sum((starts[None, :] <= positions[:, None]).astype(jnp.int32), axis=1)


def shards(frames, centers, starts):
    c = lax.axis_index("c")
    x = lax.axis_index("x")
    y = lax.axis_index("y")
    z = lax.axis_index("z")
    blocks = NZ * NX * NC
    partner = along(frames, "c", 1)
    last = frames[F - TAIL:]
    chips = ("z", "x", "c")
    tail = lax.ppermute(last, chips, [(i, i + 1) for i in range(1, blocks - 1, 2)])
    tail = tail + lax.ppermute(last, chips, [(i, i + 2) for i in range(1, blocks - 2, 2)])

    near = lax.dynamic_slice_in_dim(centers, c * (W // NC), W // NC, 0)
    sent = [lax.ppermute(near, "y", [(0, d)]) for d in range(1, NY)]

    first = (z * NX + x) * FC
    positions = first - TAIL + jnp.arange(FE, dtype=jnp.int32)
    usable = jnp.logical_and(
        segment_of(positions - LAG, starts) == segment_of(positions, starts), positions >= LAG
    ).astype(jnp.float32)[None, :] * (K * K / (blocks * F))

    where = jnp.stack([c, x]).astype(jnp.int32)
    e, mine, peers = memberships(where, frames, partner, tail, centers)
    given = jnp.where(y == 0, near, jnp.zeros_like(near))
    sent, e = lax.optimization_barrier((sent, e))
    for part in sent:
        given = given + part
    other = along(given, "c", 1)
    peers, given = lax.optimization_barrier((peers, given))
    peers = lax.all_to_all(peers, ("c", "y"), 0, 0, tiled=True)
    window = jnp.where(c == 0, jnp.concatenate([given, other]), jnp.concatenate([other, given]))
    window = window.reshape(NZ, NX, CH // NZ, D)
    distances = window_distances(where, frames, partner, tail, window, mine)
    a2, b2, pa, pb, ma, mb, home = partial_counts(distances, mine, peers, usable, e)

    via_a = along(packed(a2), "x", 1)
    via_b = along(packed(b2), "x", -1)
    up_b = along(packed(pb), "x", 1)
    down_a = along(packed(ma), "x", -1)
    up_a = along(packed(pa + opened(via_a)), "x", 1)
    down_b = along(packed(mb + opened(via_b)), "x", -1)
    low = home[:, :HALF] + opened(up_a) + opened(down_a)
    high = home[:, HALF:] + opened(up_b) + opened(down_b)
    rows = CH // (NZ * NC)
    share = packed(jnp.concatenate([low, high], axis=1)).reshape(NZ * NC, rows, KD)
    shares = opened(lax.all_to_all(share, ("z", "c"), 0, 0, tiled=True))
    summed = jnp.sum(shares.reshape(NZ, NC, rows, KD), axis=0)
    return jnp.concatenate([summed[0], summed[1]], axis=1)


def solution(mesh):
    grid = Mesh(mesh.devices.reshape(NZ, NX, NC, NY), ("z", "x", "c", "y"))
    blocks = ("z", "x", "c")
    return jax.shard_map(
        shards,
        mesh=grid,
        in_specs=(P(blocks, None), P("y", None), P()),
        out_specs=P(blocks, "y"),
        check_vma=False,
    )
```

```python
import math

import jax
import jax.numpy as jnp
from jax import lax
from jax.experimental import pallas as pl
from jax.experimental.pallas import tpu as pltpu
from jax.sharding import Mesh, PartitionSpec as P

K = 16384
W = 512
LAG = 5
D = 512
SHARPNESS = 0.03125

NZ, NX, NC, NY = 8, 4, 2, 4
F = 1024
FC = NC * F
TAIL = 128
FE = TAIL + FC
KD = 2048
FB = 256
KB = 256
NB = FC // FB
CH = W // NX
HALF = KD // 2

LOG2E = math.log2(math.e)
DECAY = -SHARPNESS * LOG2E

SENT = jnp.float16
ROOT_SCALE = 8.0


NT = (((1,), (1,)), ((), ()))
VMEM = pl.BlockSpec(memory_space=pltpu.VMEM)
ANY = pl.BlockSpec(memory_space=pl.ANY)


def member_kernel(own, partner, tail_a, tail_b, centers, e_ref, st_ref, peers_ref,
                  xs, cs, bias, u0, u1, e0, e1, sems, out_sems):
    c = lax.axis_index("c")
    copies = [
        pltpu.make_async_copy(centers.at[pl.ds(c * KD, KD)], cs, sems.at[0]),
        pltpu.make_async_copy(own, xs.at[pl.ds(TAIL + c * F, F)], sems.at[1]),
        pltpu.make_async_copy(partner, xs.at[pl.ds(TAIL + (1 - c) * F, F)], sems.at[2]),
    ]
    for copy in copies:
        copy.start()
    xs[0:TAIL, :] = tail_a[...] + tail_b[...]
    for copy in copies:
        copy.wait()
    for i in range(KD // KB):
        block = cs[i * KB:(i + 1) * KB, :].astype(jnp.float32)
        norm = jnp.sum(block * block, axis=1, keepdims=True)
        bias[i * KB:(i + 1) * KB, :] = jnp.broadcast_to(norm, (KB, 128))
    slots = (u0, e0), (u1, e1)

    def out_copy(b, slot):
        start = pl.multiple_of(b * FB, FB)
        return pltpu.make_async_copy(slots[slot][1], e_ref.at[:, pl.ds(start, FB)], out_sems.at[slot])

    def stage(new, old):
        if new is not None:
            start, width, slot = new
            u = slots[slot][0]
            xb = xs[pl.ds(start, width), :]
            xf = xb.astype(jnp.float32)
            sq = xf * xf
            part = sq[:, 0:128] + sq[:, 128:256] + sq[:, 256:384] + sq[:, 384:512]
            frame = jnp.sum(part.T, axis=0, keepdims=True)
            twice = xb * jnp.bfloat16(-2.0)
            least = None
        if old is not None:
            start_o, width_o, slot_o, keep, least_o = old
            u_o, e_o = slots[slot_o]
            total = None
        for i in range(KD // KB):
            rows = slice(i * KB, (i + 1) * KB)
            if new is not None:
                ip = lax.dot_general(cs[rows, :], twice, NT, preferred_element_type=jnp.float32)
                b = bias[rows, :]
                v = (frame + ip) + (b if width == 128 else jnp.concatenate([b] * (width // 128), axis=1))
                u[rows, 0:width] = v
                h = jnp.min(v.reshape(KB // 8, 8, width), axis=0)
                least = h if least is None else jnp.minimum(least, h)
            if old is not None:
                e = jnp.exp2((u_o[rows, 0:width_o] - least_o) * DECAY)
                t = jnp.sum(e.reshape(KB // 8, 8, width_o), axis=0)
                total = t if total is None else total + t
                if keep:
                    e_o[rows, :] = e
        if old is not None:
            total = jnp.sum(total, axis=0, keepdims=True)
            both = jnp.concatenate([least_o, total], axis=0)
            peers_ref[:, :, pl.ds(start_o, width_o)] = jnp.broadcast_to(both[None], (NC * NY, 2, width_o))
        if new is not None:
            least = jnp.min(least, axis=0, keepdims=True)
            st_ref[0:1, pl.ds(start, width)] = least
            st_ref[1:2, pl.ds(start, width)] = frame
            return least

    def at(b):
        return pl.multiple_of(TAIL + b * FB, 128)

    least = stage((0, TAIL, 1), None)
    least = stage((TAIL, FB, 0), (0, TAIL, 1, False, least))

    def step(k, least):
        for half in range(2):
            b = 2 * k + half

            @pl.when(k > 0)
            def _():
                out_copy(b - 2, half).wait()

            least = stage((at(b + 1), FB, 1 - half), (at(b), FB, half, True, least))
            out_copy(b, half).start()
        return least

    least = lax.fori_loop(0, NB // 2 - 1, step, least)
    out_copy(NB - 4, 0).wait()
    least = stage((at(NB - 1), FB, 1), (at(NB - 2), FB, 0, True, least))
    out_copy(NB - 2, 0).start()
    out_copy(NB - 3, 1).wait()
    stage(None, (at(NB - 1), FB, 1, True, least))
    out_copy(NB - 1, 1).start()
    out_copy(NB - 2, 0).wait()
    out_copy(NB - 1, 1).wait()


def memberships(own, partner, tail_a, tail_b, centers):
    return pl.pallas_call(
        member_kernel,
        in_specs=[ANY, ANY, VMEM, VMEM, ANY],
        out_specs=[ANY, VMEM, VMEM],
        out_shape=[
            jax.ShapeDtypeStruct((KD, FC), jnp.float32),
            jax.ShapeDtypeStruct((2, FE), jnp.float32),
            jax.ShapeDtypeStruct((NC * NY, 2, FE), jnp.float32),
        ],
        scratch_shapes=[
            pltpu.VMEM((FE, D), jnp.bfloat16),
            pltpu.VMEM((KD, D), jnp.bfloat16),
            pltpu.VMEM((KD, 128), jnp.float32),
            pltpu.VMEM((KD, FB), jnp.float32),
            pltpu.VMEM((KD, FB), jnp.float32),
            pltpu.VMEM((KD, FB), jnp.float32),
            pltpu.VMEM((KD, FB), jnp.float32),
            pltpu.SemaphoreType.DMA((3,)),
            pltpu.SemaphoreType.DMA((2,)),
        ],
        cost_estimate=pl.CostEstimate(flops=2 * KD * FE * D, bytes_accessed=2 * (KD * FC + KD * D + FE * D),
                                      transcendentals=KD * FE),
        name="memberships",
    )(own, partner, tail_a, tail_b, centers)


def window_kernel(own, partner, tail_a, tail_b, near, one, two, three, mine, out, twice, rows, norms):
    c = lax.axis_index("c")
    x = lax.axis_index("x")
    i = pl.program_id(0)

    @pl.when(i == 0)
    def _():
        minus_two = jnp.bfloat16(-2.0)
        twice[0:TAIL, :] = (tail_a[...] + tail_b[...]) * minus_two
        for ref, start in ((own, TAIL + c * F), (partner, TAIL + (1 - c) * F)):
            twice[pl.ds(pl.multiple_of(start, 128), F), :] = ref[...] * minus_two
        here = jnp.where(lax.axis_index("y") == 0, 1.0, 0.0).astype(jnp.bfloat16)
        part = CH // NZ
        for d in range(NX):
            turn = lax.rem(x + d, NX)
            for s in range(NZ):
                at = pl.ds(pl.multiple_of((s * NX + turn) * part, part), part)
                to = d * CH + s * part
                rows[to:to + part, :] = near[at, :] * here + ((one[at, :] + two[at, :]) + three[at, :])
            rf = rows[d * CH:(d + 1) * CH, :].astype(jnp.float32)
            norm = jnp.sum(rf * rf, axis=1, keepdims=True)
            norms[d * CH:(d + 1) * CH, :] = jnp.broadcast_to(norm, (CH, 128))

    ip = lax.dot_general(rows[...], twice[pl.ds(pl.multiple_of(i * FB, FB), FB), :], NT,
                         preferred_element_type=jnp.float32)
    norm = norms[...]
    out[...] = (mine[1:2, :] + ip) + jnp.concatenate([norm, norm], axis=1)


def window_distances(own, partner, tail_a, tail_b, near, sent, mine):
    blocks = pl.cdiv(FE, FB)
    return pl.pallas_call(
        window_kernel,
        grid=(blocks,),
        in_specs=[VMEM] * 8 + [pl.BlockSpec((2, FB), lambda i: (0, i))],
        out_specs=pl.BlockSpec((W, FB), lambda i: (0, i)),
        out_shape=jax.ShapeDtypeStruct((W, FE), jnp.float32),
        scratch_shapes=[
            pltpu.VMEM((blocks * FB, D), jnp.bfloat16),
            pltpu.VMEM((W, D), jnp.bfloat16),
            pltpu.VMEM((W, 128), jnp.float32),
        ],
        cost_estimate=pl.CostEstimate(flops=2 * W * FE * D, bytes_accessed=4 * W * FE, transcendentals=0),
        name="window_distances",
    )(own, partner, tail_a, tail_b, near, *sent, mine)


def count_kernel(distances, mine, peers, starts, e_ref, a2, b2, pa, pb, ma, mb, home, lead, factor, level):
    step = pl.program_id(0)
    j = step - NX

    @pl.when(step == 0)
    def _():
        mins = peers[:, 0, :]
        least = jnp.min(mins, axis=0, keepdims=True)
        total = jnp.sum(peers[:, 1, :] * jnp.exp2((mins - least) * DECAY), axis=0, keepdims=True)
        inverse = 1.0 / total
        lag_scale = jnp.exp2((mine[0:1, :] - least) * DECAY) * inverse
        factor[...] = lag_scale[:, TAIL:]
        level[0:1, :] = least
        first = (lax.axis_index("z") * NX + lax.axis_index("x")) * FC
        lag = first - TAIL + lax.broadcasted_iota(jnp.int32, (1, FE), 1)
        begins = jnp.logical_and(starts[...] <= lag, starts[...] > lag - LAG)
        begun = jnp.sum(jnp.where(begins, 1.0, 0.0), axis=0, keepdims=True)
        usable = jnp.where(jnp.logical_and(begun == 0.0, lag >= LAG), K * K / (NZ * NX * FC), 0.0)
        level[1:2, :] = inverse * pltpu.roll(usable, FE - LAG, 1)

    @pl.when(step < NX)
    def _():
        for r in range(0, CH, 64):
            m = jnp.exp2((distances[r:r + 64, :] - level[0:1, :]) * DECAY) * level[1:2, :]
            at = pl.ds(pl.multiple_of(step * CH + r, 64), 64)
            lead[at, :] = pltpu.roll(m, LAG, 1)[:, TAIL:].astype(jnp.bfloat16)

    def part_of():
        member = (e_ref[...] * factor[...]).astype(jnp.bfloat16)
        part = lax.dot_general(lead[...], member, NT, preferred_element_type=jnp.float32)
        home[...] = part[0:CH]
        return part[CH:2 * CH], part[2 * CH:3 * CH], part[3 * CH:4 * CH]

    @pl.when(jnp.logical_and(j >= 0, j < NB // 2))
    def _():
        pa[...], a2[...], ma[...] = part_of()

    @pl.when(j >= NB // 2)
    def _():
        pb[...], b2[...], mb[...] = part_of()


def partial_counts(distances, mine, peers, starts, e):
    jb = KD // NB
    low = pl.BlockSpec((CH, jb), lambda s: (0, jnp.clip(s - NX, 0, NB // 2 - 1)))
    high = pl.BlockSpec((CH, jb), lambda s: (0, jnp.maximum(s - NX - NB // 2, 0)))
    f32 = jnp.float32
    half = jax.ShapeDtypeStruct((CH, HALF), f32)
    return pl.pallas_call(
        count_kernel,
        grid=(NX + NB,),
        in_specs=[pl.BlockSpec((CH, FE), lambda s: (jnp.minimum(s, NX - 1), 0))] + [VMEM] * 3
        + [pl.BlockSpec((jb, FC), lambda s: (jnp.maximum(s - NX, 0), 0))],
        out_specs=[low, high, low, high, low, high, pl.BlockSpec((CH, jb), lambda s: (0, jnp.maximum(s - NX, 0)))],
        out_shape=[half] * 6 + [jax.ShapeDtypeStruct((CH, KD), f32)],
        scratch_shapes=[pltpu.VMEM((W, FC), jnp.bfloat16), pltpu.VMEM((1, FC), f32), pltpu.VMEM((2, FE), f32)],
        cost_estimate=pl.CostEstimate(flops=2 * W * FC * KD, bytes_accessed=4 * FC * KD + 4 * W * FE,
                                      transcendentals=W * FE),
        name="counts",
    )(distances, mine, peers, starts, e)


def along(block, axis, distance):
    n = lax.axis_size(axis)
    return lax.ppermute(block, axis, [(i, (i + distance) % n) for i in range(n)])


def packed(counts):
    return (jnp.sqrt(counts) * ROOT_SCALE).astype(SENT)


def opened(message):
    root = message.astype(jnp.float32) * (1.0 / ROOT_SCALE)
    return root * root


def shards(frames, centers, starts):
    partner = along(frames, "c", 1)
    last = frames[F - TAIL:]
    blocks = NZ * NX * NC
    chips = ("z", "x", "c")
    tail_a = lax.ppermute(last, chips, [(i, i + 1) for i in range(1, blocks - 1, 2)])
    tail_b = lax.ppermute(last, chips, [(i, i + 2) for i in range(1, blocks - 2, 2)])
    near = centers[:W]
    sent = [lax.ppermute(near, "y", [(0, d)]) for d in (2, 1, 3)]

    e, mine, peers = memberships(frames, partner, tail_a, tail_b, centers)
    peers = lax.all_to_all(peers, ("c", "y"), 0, 0, tiled=True)
    distances = window_distances(frames, partner, tail_a, tail_b, near, sent, mine)
    a2, b2, pa, pb, ma, mb, home = partial_counts(distances, mine, peers, starts[:, None], e)

    via_a = along(packed(a2), "x", 1)
    via_b = along(packed(b2), "x", -1)
    up_b = along(packed(pb), "x", 1)
    down_a = along(packed(ma), "x", -1)
    up_a = along(packed(pa + opened(via_a)), "x", 1)
    down_b = along(packed(mb + opened(via_b)), "x", -1)
    low = home[:, :HALF] + opened(up_a) + opened(down_a)
    high = home[:, HALF:] + opened(up_b) + opened(down_b)
    rows = CH // (NZ * NC)
    share = packed(jnp.concatenate([low, high], axis=1)).reshape(NZ * NC, rows, KD)
    shares = opened(lax.all_to_all(share, ("z", "c"), 0, 0, tiled=True))
    summed = jnp.sum(shares.reshape(NZ, NC, rows, KD), axis=0)
    return jnp.concatenate([summed[0], summed[1]], axis=1)


def solution(mesh):
    grid = Mesh(mesh.devices.reshape(NZ, NX, NC, NY), ("z", "x", "c", "y"))
    blocks = ("z", "x", "c")
    return jax.shard_map(
        shards,
        mesh=grid,
        in_specs=(P(blocks, None), P("y", None), P()),
        out_specs=P(blocks, "y"),
        check_vma=False,
    )
```

```python
import math

import jax
import jax.numpy as jnp
from jax import lax
from jax.experimental import pallas as pl
from jax.experimental.pallas import tpu as pltpu
from jax.sharding import Mesh, PartitionSpec as P

K = 16384
W = 512
LAG = 5
D = 512
SHARPNESS = 0.03125

NZ, NX, NC, NY = 8, 4, 2, 4
F = 1024
FC = NC * F
TAIL = 128
FE = TAIL + FC
KD = 2048
FB = 256
KB = 256
NB = FC // FB
CH = W // NX
HALF = KD // 2

LOG2E = math.log2(math.e)
DECAY = -SHARPNESS * LOG2E

SENT = jnp.float16
ROOT_SCALE = 8.0


NT = (((1,), (1,)), ((), ()))
VMEM = pl.BlockSpec(memory_space=pltpu.VMEM)
ANY = pl.BlockSpec(memory_space=pl.ANY)


def member_kernel(own, partner, tail_a, tail_b, centers, e_ref, st_ref, peers_ref, xs_out,
                  xs, cs, bias, u0, u1, e0, e1, sems, out_sems):
    c = lax.axis_index("c")
    copies = [
        pltpu.make_async_copy(centers.at[pl.ds(c * KD, KD)], cs, sems.at[0]),
        pltpu.make_async_copy(own, xs.at[pl.ds(TAIL + c * F, F)], sems.at[1]),
        pltpu.make_async_copy(partner, xs.at[pl.ds(TAIL + (1 - c) * F, F)], sems.at[2]),
    ]
    for copy in copies:
        copy.start()
    xs[0:TAIL, :] = tail_a[...] + tail_b[...]
    for copy in copies:
        copy.wait()
    keep_xs = pltpu.make_async_copy(xs, xs_out, sems.at[3])
    keep_xs.start()
    for i in range(KD // KB):
        block = cs[i * KB:(i + 1) * KB, :].astype(jnp.float32)
        norm = jnp.sum(block * block, axis=1, keepdims=True)
        bias[i * KB:(i + 1) * KB, :] = jnp.broadcast_to(norm, (KB, 128))
    slots = (u0, e0), (u1, e1)

    def out_copy(b, slot):
        start = pl.multiple_of(b * FB, FB)
        return pltpu.make_async_copy(slots[slot][1], e_ref.at[:, pl.ds(start, FB)], out_sems.at[slot])

    def stage(new, old):
        if new is not None:
            start, width, slot = new
            u = slots[slot][0]
            xb = xs[pl.ds(start, width), :]
            xf = xb.astype(jnp.float32)
            sq = xf * xf
            part = sq[:, 0:128] + sq[:, 128:256] + sq[:, 256:384] + sq[:, 384:512]
            frame = jnp.sum(part.T, axis=0, keepdims=True)
            twice = xb * jnp.bfloat16(-2.0)
            least = None
        if old is not None:
            start_o, width_o, slot_o, keep, least_o = old
            u_o, e_o = slots[slot_o]
            total = None
        for i in range(KD // KB):
            rows = slice(i * KB, (i + 1) * KB)
            if new is not None:
                ip = lax.dot_general(cs[rows, :], twice, NT, preferred_element_type=jnp.float32)
                b = bias[rows, :]
                v = (frame + ip) + (b if width == 128 else jnp.concatenate([b] * (width // 128), axis=1))
                u[rows, 0:width] = v
                h = jnp.min(v.reshape(KB // 8, 8, width), axis=0)
                least = h if least is None else jnp.minimum(least, h)
            if old is not None:
                e = jnp.exp2((u_o[rows, 0:width_o] - least_o) * DECAY)
                t = jnp.sum(e.reshape(KB // 8, 8, width_o), axis=0)
                total = t if total is None else total + t
                if keep:
                    e_o[rows, :] = e
        if old is not None:
            total = jnp.sum(total, axis=0, keepdims=True)
            both = jnp.concatenate([least_o, total], axis=0)
            peers_ref[:, :, pl.ds(start_o, width_o)] = jnp.broadcast_to(both[None], (NC * NY, 2, width_o))
        if new is not None:
            least = jnp.min(least, axis=0, keepdims=True)
            st_ref[0:1, pl.ds(start, width)] = least
            st_ref[1:2, pl.ds(start, width)] = frame
            return least

    def at(b):
        return pl.multiple_of(TAIL + b * FB, 128)

    least = stage((0, TAIL, 1), None)
    least = stage((TAIL, FB, 0), (0, TAIL, 1, False, least))

    def step(k, least):
        for half in range(2):
            b = 2 * k + half

            @pl.when(k > 0)
            def _():
                out_copy(b - 2, half).wait()

            least = stage((at(b + 1), FB, 1 - half), (at(b), FB, half, True, least))
            out_copy(b, half).start()
        return least

    least = lax.fori_loop(0, NB // 2 - 1, step, least)
    out_copy(NB - 4, 0).wait()
    least = stage((at(NB - 1), FB, 1), (at(NB - 2), FB, 0, True, least))
    out_copy(NB - 2, 0).start()
    out_copy(NB - 3, 1).wait()
    stage(None, (at(NB - 1), FB, 1, True, least))
    out_copy(NB - 1, 1).start()
    out_copy(NB - 2, 0).wait()
    out_copy(NB - 1, 1).wait()
    keep_xs.wait()


def memberships(own, partner, tail_a, tail_b, centers):
    return pl.pallas_call(
        member_kernel,
        in_specs=[ANY, ANY, VMEM, VMEM, ANY],
        out_specs=[ANY, VMEM, VMEM, ANY],
        out_shape=[
            jax.ShapeDtypeStruct((KD, FC), jnp.float32),
            jax.ShapeDtypeStruct((2, FE), jnp.float32),
            jax.ShapeDtypeStruct((NC * NY, 2, FE), jnp.float32),
            jax.ShapeDtypeStruct((FE, D), jnp.bfloat16),
        ],
        scratch_shapes=[
            pltpu.VMEM((FE, D), jnp.bfloat16),
            pltpu.VMEM((KD, D), jnp.bfloat16),
            pltpu.VMEM((KD, 128), jnp.float32),
            pltpu.VMEM((KD, FB), jnp.float32),
            pltpu.VMEM((KD, FB), jnp.float32),
            pltpu.VMEM((KD, FB), jnp.float32),
            pltpu.VMEM((KD, FB), jnp.float32),
            pltpu.SemaphoreType.DMA((4,)),
            pltpu.SemaphoreType.DMA((2,)),
        ],
        cost_estimate=pl.CostEstimate(flops=2 * KD * FE * D, bytes_accessed=2 * (KD * FC + KD * D + FE * D),
                                      transcendentals=KD * FE),
        name="memberships",
    )(own, partner, tail_a, tail_b, centers)


def window_kernel(near, one, two, three, xs, mine, out, rows, twice, norms, sems):
    x = lax.axis_index("x")
    y = lax.axis_index("y")

    @pl.when(pl.program_id(0) == 0)
    def _():
        for holder, ref in enumerate((near, one, two, three)):
            @pl.when(y == holder)
            def _():
                copies = [
                    pltpu.make_async_copy(ref.at[:, lax.rem(x + d, NX)], rows.at[d], sems.at[d]) for d in range(NX)
                ]
                for copy in copies:
                    copy.start()
                for copy in copies:
                    copy.wait()

        for d in range(NX):
            part = rows[d].reshape(CH, D)
            pf = part.astype(jnp.float32)
            norm = jnp.sum(pf * pf, axis=1, keepdims=True)
            norms[d * CH:(d + 1) * CH, :] = jnp.broadcast_to(norm, (CH, 128))
            twice[d * CH:(d + 1) * CH, :] = part * jnp.bfloat16(-2.0)

    ip = lax.dot_general(twice[...], xs[...], NT, preferred_element_type=jnp.float32)
    norm = norms[...]
    out[...] = (mine[1:2, :] + ip) + jnp.concatenate([norm, norm], axis=1)


def window_distances(windows, xs, mine):
    windows = [w.reshape(NZ, NX, CH // NZ, D) for w in windows]
    return pl.pallas_call(
        window_kernel,
        grid=(pl.cdiv(FE, FB),),
        in_specs=[ANY] * NY + [pl.BlockSpec((FB, D), lambda i: (i, 0)), pl.BlockSpec((2, FB), lambda i: (0, i))],
        out_specs=pl.BlockSpec((W, FB), lambda i: (0, i)),
        out_shape=jax.ShapeDtypeStruct((W, FE), jnp.float32),
        scratch_shapes=[
            pltpu.VMEM((NX, NZ, CH // NZ, D), jnp.bfloat16),
            pltpu.VMEM((W, D), jnp.bfloat16),
            pltpu.VMEM((W, 128), jnp.float32),
            pltpu.SemaphoreType.DMA((NX,)),
        ],
        cost_estimate=pl.CostEstimate(flops=2 * W * FE * D, bytes_accessed=4 * W * FE, transcendentals=0),
        name="window_distances",
    )(*windows, xs, mine)


def count_kernel(distances, mine, peers, starts, e_ref, a2, b2, pa, pb, ma, mb, home, lead, factor, level):
    step = pl.program_id(0)
    j = step - NX

    @pl.when(step == 0)
    def _():
        mins = peers[:, 0, :]
        least = jnp.min(mins, axis=0, keepdims=True)
        total = jnp.sum(peers[:, 1, :] * jnp.exp2((mins - least) * DECAY), axis=0, keepdims=True)
        inverse = 1.0 / total
        lag_scale = jnp.exp2((mine[0:1, :] - least) * DECAY) * inverse
        factor[...] = lag_scale[:, TAIL:]
        level[0:1, :] = least
        first = (lax.axis_index("z") * NX + lax.axis_index("x")) * FC
        lag = first - TAIL + lax.broadcasted_iota(jnp.int32, (1, FE), 1)
        begins = jnp.logical_and(starts[...] <= lag, starts[...] > lag - LAG)
        begun = jnp.sum(jnp.where(begins, 1.0, 0.0), axis=0, keepdims=True)
        usable = jnp.where(jnp.logical_and(begun == 0.0, lag >= LAG), K * K / (NZ * NX * FC), 0.0)
        level[1:2, :] = inverse * pltpu.roll(usable, FE - LAG, 1)

    @pl.when(step < NX)
    def _():
        for r in range(0, CH, 64):
            m = jnp.exp2((distances[r:r + 64, :] - level[0:1, :]) * DECAY) * level[1:2, :]
            at = pl.ds(pl.multiple_of(step * CH + r, 64), 64)
            lead[at, :] = pltpu.roll(m, LAG, 1)[:, TAIL:].astype(jnp.bfloat16)

    def part_of():
        member = (e_ref[...] * factor[...]).astype(jnp.bfloat16)
        part = lax.dot_general(lead[...], member, NT, preferred_element_type=jnp.float32)
        home[...] = part[0:CH]
        return part[CH:2 * CH], part[2 * CH:3 * CH], part[3 * CH:4 * CH]

    @pl.when(jnp.logical_and(j >= 0, j < NB // 2))
    def _():
        pa[...], a2[...], ma[...] = part_of()

    @pl.when(j >= NB // 2)
    def _():
        pb[...], b2[...], mb[...] = part_of()


def partial_counts(distances, mine, peers, starts, e):
    jb = KD // NB
    low = pl.BlockSpec((CH, jb), lambda s: (0, jnp.clip(s - NX, 0, NB // 2 - 1)))
    high = pl.BlockSpec((CH, jb), lambda s: (0, jnp.maximum(s - NX - NB // 2, 0)))
    f32 = jnp.float32
    half = jax.ShapeDtypeStruct((CH, HALF), f32)
    return pl.pallas_call(
        count_kernel,
        grid=(NX + NB,),
        in_specs=[pl.BlockSpec((CH, FE), lambda s: (jnp.minimum(s, NX - 1), 0))] + [VMEM] * 3
        + [pl.BlockSpec((jb, FC), lambda s: (jnp.maximum(s - NX, 0), 0))],
        out_specs=[low, high, low, high, low, high, pl.BlockSpec((CH, jb), lambda s: (0, jnp.maximum(s - NX, 0)))],
        out_shape=[half] * 6 + [jax.ShapeDtypeStruct((CH, KD), f32)],
        scratch_shapes=[pltpu.VMEM((W, FC), jnp.bfloat16), pltpu.VMEM((1, FC), f32), pltpu.VMEM((2, FE), f32)],
        cost_estimate=pl.CostEstimate(flops=2 * W * FC * KD, bytes_accessed=4 * FC * KD + 4 * W * FE,
                                      transcendentals=W * FE),
        name="counts",
    )(distances, mine, peers, starts, e)


def along(block, axis, distance):
    n = lax.axis_size(axis)
    return lax.ppermute(block, axis, [(i, (i + distance) % n) for i in range(n)])


def packed(counts):
    return (jnp.sqrt(counts) * ROOT_SCALE).astype(SENT)


def opened(message):
    root = message.astype(jnp.float32) * (1.0 / ROOT_SCALE)
    return root * root


def shards(frames, centers, starts):
    partner = along(frames, "c", 1)
    last = frames[F - TAIL:]
    blocks = NZ * NX * NC
    chips = ("z", "x", "c")
    tail_a = lax.ppermute(last, chips, [(i, i + 1) for i in range(1, blocks - 1, 2)])
    tail_b = lax.ppermute(last, chips, [(i, i + 2) for i in range(1, blocks - 2, 2)])
    near = centers[:W]
    windows = [near] + [lax.ppermute(near, "y", [(0, d)]) for d in range(1, NY)]

    e, mine, peers, xs = memberships(frames, partner, tail_a, tail_b, centers)
    peers = lax.all_to_all(peers, ("c", "y"), 0, 0, tiled=True)
    distances = window_distances(windows, xs, mine)
    a2, b2, pa, pb, ma, mb, home = partial_counts(distances, mine, peers, starts[:, None], e)

    via_a = along(packed(a2), "x", 1)
    via_b = along(packed(b2), "x", -1)
    up_b = along(packed(pb), "x", 1)
    down_a = along(packed(ma), "x", -1)
    up_a = along(packed(pa + opened(via_a)), "x", 1)
    down_b = along(packed(mb + opened(via_b)), "x", -1)
    low = home[:, :HALF] + opened(up_a) + opened(down_a)
    high = home[:, HALF:] + opened(up_b) + opened(down_b)
    rows = CH // (NZ * NC)
    share = packed(jnp.concatenate([low, high], axis=1)).reshape(NZ * NC, rows, KD)
    shares = opened(lax.all_to_all(share, ("z", "c"), 0, 0, tiled=True))
    summed = jnp.sum(shares.reshape(NZ, NC, rows, KD), axis=0)
    return jnp.concatenate([summed[0], summed[1]], axis=1)


def solution(mesh):
    grid = Mesh(mesh.devices.reshape(NZ, NX, NC, NY), ("z", "x", "c", "y"))
    blocks = ("z", "x", "c")
    return jax.shard_map(
        shards,
        mesh=grid,
        in_specs=(P(blocks, None), P("y", None), P()),
        out_specs=P(blocks, "y"),
        check_vma=False,
    )
```

```python
import math

import jax
import jax.numpy as jnp
from jax import lax
from jax.experimental import pallas as pl
from jax.experimental.pallas import tpu as pltpu
from jax.sharding import Mesh, PartitionSpec as P

K = 16384
W = 512
LAG = 5
D = 512
SHARPNESS = 0.03125

NZ, NX, NC, NY = 8, 4, 2, 4
F = 1024
FC = NC * F
TAIL = 128
FE = TAIL + FC
KD = 2048
FB = 256
KB = 256
NB = FC // FB
CH = W // NX
HALF = KD // 2

LOG2E = math.log2(math.e)
DECAY = -SHARPNESS * LOG2E

SENT = jnp.float16
ROOT_SCALE = 8.0


NT = (((1,), (1,)), ((), ()))
VMEM = pl.BlockSpec(memory_space=pltpu.VMEM)
ANY = pl.BlockSpec(memory_space=pl.ANY)


def member_kernel(own, partner, tail_a, tail_b, centers, e_ref, st_ref, peers_ref, xs_out,
                  xs, cs, bias, u0, u1, e0, e1, sems, out_sems):
    c = lax.axis_index("c")
    copies = [
        pltpu.make_async_copy(centers.at[pl.ds(c * KD, KD)], cs, sems.at[0]),
        pltpu.make_async_copy(own, xs.at[pl.ds(TAIL + c * F, F)], sems.at[1]),
        pltpu.make_async_copy(partner, xs.at[pl.ds(TAIL + (1 - c) * F, F)], sems.at[2]),
    ]
    for copy in copies:
        copy.start()
    xs[0:TAIL, :] = tail_a[...] + tail_b[...]
    for copy in copies:
        copy.wait()
    keep_xs = pltpu.make_async_copy(xs, xs_out, sems.at[3])
    keep_xs.start()
    for i in range(KD // KB):
        block = cs[i * KB:(i + 1) * KB, :].astype(jnp.float32)
        norm = jnp.sum(block * block, axis=1, keepdims=True)
        bias[i * KB:(i + 1) * KB, :] = jnp.broadcast_to(norm, (KB, 128))
    slots = (u0, e0), (u1, e1)

    def out_copy(b, slot):
        start = pl.multiple_of(b * FB, FB)
        return pltpu.make_async_copy(slots[slot][1], e_ref.at[:, pl.ds(start, FB)], out_sems.at[slot])

    def stage(new, old):
        if new is not None:
            start, width, slot = new
            u = slots[slot][0]
            xb = xs[pl.ds(start, width), :]
            xf = xb.astype(jnp.float32)
            sq = xf * xf
            part = sq[:, 0:128] + sq[:, 128:256] + sq[:, 256:384] + sq[:, 384:512]
            frame = jnp.sum(part.T, axis=0, keepdims=True)
            twice = xb * jnp.bfloat16(-2.0)
            least = None
        if old is not None:
            start_o, width_o, slot_o, keep, least_o = old
            u_o, e_o = slots[slot_o]
            total = None
        for i in range(KD // KB):
            rows = slice(i * KB, (i + 1) * KB)
            if new is not None:
                ip = lax.dot_general(cs[rows, :], twice, NT, preferred_element_type=jnp.float32)
                b = bias[rows, :]
                v = (frame + ip) + (b if width == 128 else jnp.concatenate([b] * (width // 128), axis=1))
                u[rows, 0:width] = v
                h = jnp.min(v.reshape(KB // 8, 8, width), axis=0)
                least = h if least is None else jnp.minimum(least, h)
            if old is not None:
                e = jnp.exp2((u_o[rows, 0:width_o] - least_o) * DECAY)
                t = jnp.sum(e.reshape(KB // 8, 8, width_o), axis=0)
                total = t if total is None else total + t
                if keep:
                    e_o[rows, :] = e
        if old is not None:
            total = jnp.sum(total, axis=0, keepdims=True)
            both = jnp.concatenate([least_o, total], axis=0)
            peers_ref[:, :, pl.ds(start_o, width_o)] = jnp.broadcast_to(both[None], (NC * NY, 2, width_o))
        if new is not None:
            least = jnp.min(least, axis=0, keepdims=True)
            st_ref[0:1, pl.ds(start, width)] = least
            st_ref[1:2, pl.ds(start, width)] = frame
            return least

    def at(b):
        return pl.multiple_of(TAIL + b * FB, 128)

    least = stage((0, TAIL, 1), None)
    least = stage((TAIL, FB, 0), (0, TAIL, 1, False, least))

    def step(k, least):
        for half in range(2):
            b = 2 * k + half

            @pl.when(k > 0)
            def _():
                out_copy(b - 2, half).wait()

            least = stage((at(b + 1), FB, 1 - half), (at(b), FB, half, True, least))
            out_copy(b, half).start()
        return least

    least = lax.fori_loop(0, NB // 2 - 1, step, least)
    out_copy(NB - 4, 0).wait()
    least = stage((at(NB - 1), FB, 1), (at(NB - 2), FB, 0, True, least))
    out_copy(NB - 2, 0).start()
    out_copy(NB - 3, 1).wait()
    stage(None, (at(NB - 1), FB, 1, True, least))
    out_copy(NB - 1, 1).start()
    out_copy(NB - 2, 0).wait()
    out_copy(NB - 1, 1).wait()
    keep_xs.wait()


def memberships(own, partner, tail_a, tail_b, centers):
    return pl.pallas_call(
        member_kernel,
        in_specs=[ANY, ANY, VMEM, VMEM, ANY],
        out_specs=[ANY, VMEM, VMEM, ANY],
        out_shape=[
            jax.ShapeDtypeStruct((KD, FC), jnp.float32),
            jax.ShapeDtypeStruct((2, FE), jnp.float32),
            jax.ShapeDtypeStruct((NC * NY, 2, FE), jnp.float32),
            jax.ShapeDtypeStruct((FE, D), jnp.bfloat16),
        ],
        scratch_shapes=[
            pltpu.VMEM((FE, D), jnp.bfloat16),
            pltpu.VMEM((KD, D), jnp.bfloat16),
            pltpu.VMEM((KD, 128), jnp.float32),
            pltpu.VMEM((KD, FB), jnp.float32),
            pltpu.VMEM((KD, FB), jnp.float32),
            pltpu.VMEM((KD, FB), jnp.float32),
            pltpu.VMEM((KD, FB), jnp.float32),
            pltpu.SemaphoreType.DMA((4,)),
            pltpu.SemaphoreType.DMA((2,)),
        ],
        cost_estimate=pl.CostEstimate(flops=2 * KD * FE * D, bytes_accessed=2 * (KD * FC + KD * D + FE * D),
                                      transcendentals=KD * FE),
        name="memberships",
    )(own, partner, tail_a, tail_b, centers)


def window_kernel(near, one, two, three, xs, mine, out, rows, twice, frames, dist, sems):
    x = lax.axis_index("x")
    y = lax.axis_index("y")
    load = pltpu.make_async_copy(xs, frames, sems.at[NX])
    load.start()
    for holder, ref in enumerate((near, one, two, three)):
        @pl.when(y == holder)
        def _():
            for d in range(NX):
                pltpu.make_async_copy(ref.at[:, lax.rem(x + d, NX)], rows.at[d], sems.at[d]).start()

    for d in range(NX):
        pltpu.make_async_copy(near.at[:, 0], rows.at[d], sems.at[d]).wait()
    norms = []
    for d in range(NX):
        part = rows[d].reshape(CH, D)
        pf = part.astype(jnp.float32)
        norms.append(jnp.sum(pf * pf, axis=1, keepdims=True))
        twice[d * CH:(d + 1) * CH, :] = part * jnp.bfloat16(-2.0)
    norm = jnp.concatenate(norms, axis=0)
    load.wait()
    stores = []
    for k, (start, stop) in enumerate(CUTS):
        ip = lax.dot_general(twice[...], frames[start:stop, :], NT, preferred_element_type=jnp.float32)
        dist[:, start:stop] = (mine[1:2, start:stop] + ip) + norm
        stores.append(pltpu.make_async_copy(dist.at[:, start:stop], out.at[:, start:stop], sems.at[NX + 1 + k]))
        stores[-1].start()
    for store in stores:
        store.wait()


CUTS = ((0, 640), (640, 1152), (1152, 1664), (1664, 2176))


def window_distances(windows, xs, mine):
    windows = [w.reshape(NZ, NX, CH // NZ, D) for w in windows]
    return pl.pallas_call(
        window_kernel,
        in_specs=[ANY] * NY + [ANY, VMEM],
        out_specs=ANY,
        out_shape=jax.ShapeDtypeStruct((W, FE), jnp.float32),
        scratch_shapes=[
            pltpu.VMEM((NX, NZ, CH // NZ, D), jnp.bfloat16),
            pltpu.VMEM((W, D), jnp.bfloat16),
            pltpu.VMEM((FE, D), jnp.bfloat16),
            pltpu.VMEM((W, FE), jnp.float32),
            pltpu.SemaphoreType.DMA((NX + 1 + len(CUTS),)),
        ],
        cost_estimate=pl.CostEstimate(flops=2 * W * FE * D, bytes_accessed=4 * W * FE, transcendentals=0),
        name="window_distances",
    )(*windows, xs, mine)


JB = 512
NJ = KD // JB


def count_kernel(distances, mine, peers, starts, e, a2, b2, pa, pb, ma, mb, home,
                 dist, lead, ebuf, obuf, in_sems, e_sems, out_sems):
    loads = [
        pltpu.make_async_copy(distances.at[pl.ds(d * CH, CH)], dist.at[pl.ds(d * CH, CH)], in_sems.at[d])
        for d in range(NX)
    ]
    e_loads = [
        pltpu.make_async_copy(e.at[pl.ds(b * JB, JB)], ebuf.at[b % 2], e_sems.at[b % 2]) for b in range(NJ)
    ]
    for load in loads + e_loads[:2]:
        load.start()

    mins = peers[:, 0, :]
    least = jnp.min(mins, axis=0, keepdims=True)
    total = jnp.sum(peers[:, 1, :] * jnp.exp2((mins - least) * DECAY), axis=0, keepdims=True)
    inverse = 1.0 / total
    factor = (jnp.exp2((mine[0:1, :] - least) * DECAY) * inverse)[:, TAIL:]
    first = (lax.axis_index("z") * NX + lax.axis_index("x")) * FC
    lag = first - TAIL + lax.broadcasted_iota(jnp.int32, (1, FE), 1)
    n = starts.shape[1]
    square = lax.broadcasted_iota(jnp.int32, (n, n), 0) == lax.broadcasted_iota(jnp.int32, (n, n), 1)
    begin = jnp.sum(jnp.where(square, starts[...].astype(jnp.float32), 0.0), axis=1, keepdims=True).astype(jnp.int32)
    begins = jnp.logical_and(begin <= lag, begin > lag - LAG)
    begun = jnp.sum(jnp.where(begins, 1.0, 0.0), axis=0, keepdims=True)
    usable = jnp.where(jnp.logical_and(begun == 0.0, lag >= LAG), K * K / (NZ * NX * FC), 0.0)
    scale = inverse * pltpu.roll(usable, FE - LAG, 1)

    for d in range(NX):
        loads[d].wait()
        for r in range(d * CH, (d + 1) * CH, 64):
            m = jnp.exp2((dist[r:r + 64, :] - least) * DECAY) * scale
            lead[r:r + 64, :] = pltpu.roll(m, LAG, 1)[:, TAIL:].astype(jnp.bfloat16)

    stores = []
    for b in range(NJ):
        slot = b % 2
        e_loads[b].wait()
        if b >= 2:
            for store in stores[b - 2]:
                store.wait()
        for q in range(0, JB, FB):
            member = (ebuf[slot, q:q + FB, :] * factor).astype(jnp.bfloat16)
            obuf[slot, :, q:q + FB] = lax.dot_general(lead[...], member, NT, preferred_element_type=jnp.float32)
        into = (pa, a2, ma) if b < NJ // 2 else (pb, b2, mb)
        at = pl.ds((b % (NJ // 2)) * JB, JB)
        targets = [home.at[:, pl.ds(b * JB, JB)]] + [ref.at[:, at] for ref in into]
        stores.append([
            pltpu.make_async_copy(obuf.at[slot, pl.ds(k * CH, CH)], target, out_sems.at[slot, k])
            for k, target in enumerate(targets)
        ])
        for store in stores[b]:
            store.start()
        if b + 2 < NJ:
            e_loads[b + 2].start()
    for store in stores[NJ - 2] + stores[NJ - 1]:
        store.wait()


def partial_counts(distances, mine, peers, starts, e):
    f32 = jnp.float32
    half = jax.ShapeDtypeStruct((CH, HALF), f32)
    return pl.pallas_call(
        count_kernel,
        in_specs=[ANY] + [VMEM] * 3 + [ANY],
        out_specs=[ANY] * 7,
        out_shape=[half] * 6 + [jax.ShapeDtypeStruct((CH, KD), f32)],
        scratch_shapes=[
            pltpu.VMEM((W, FE), f32),
            pltpu.VMEM((W, FC), jnp.bfloat16),
            pltpu.VMEM((2, JB, FC), f32),
            pltpu.VMEM((2, W, JB), f32),
            pltpu.SemaphoreType.DMA((NX,)),
            pltpu.SemaphoreType.DMA((2,)),
            pltpu.SemaphoreType.DMA((2, NX)),
        ],
        cost_estimate=pl.CostEstimate(flops=2 * W * FC * KD, bytes_accessed=4 * FC * KD + 4 * W * FE,
                                      transcendentals=W * FE),
        name="counts",
    )(distances, mine, peers, starts, e)


def along(block, axis, distance):
    n = lax.axis_size(axis)
    return lax.ppermute(block, axis, [(i, (i + distance) % n) for i in range(n)])


def packed(counts):
    return (jnp.sqrt(counts) * ROOT_SCALE).astype(SENT)


def opened(message):
    root = message.astype(jnp.float32) * (1.0 / ROOT_SCALE)
    return root * root


def shards(frames, centers, starts):
    partner = along(frames, "c", 1)
    last = frames[F - TAIL:]
    blocks = NZ * NX * NC
    chips = ("z", "x", "c")
    tail_a = lax.ppermute(last, chips, [(i, i + 1) for i in range(1, blocks - 1, 2)])
    tail_b = lax.ppermute(last, chips, [(i, i + 2) for i in range(1, blocks - 2, 2)])
    near = centers[:W]
    windows = [near] + [lax.ppermute(near, "y", [(0, d)]) for d in range(1, NY)]

    e, mine, peers, xs = memberships(frames, partner, tail_a, tail_b, centers)
    peers = lax.all_to_all(peers, ("c", "y"), 0, 0, tiled=True)
    distances = window_distances(windows, xs, mine)
    a2, b2, pa, pb, ma, mb, home = partial_counts(distances, mine, peers, starts[None, :], e)

    via_a = along(packed(a2), "x", 1)
    via_b = along(packed(b2), "x", -1)
    up_b = along(packed(pb), "x", 1)
    down_a = along(packed(ma), "x", -1)
    up_a = along(packed(pa + opened(via_a)), "x", 1)
    down_b = along(packed(mb + opened(via_b)), "x", -1)
    low = home[:, :HALF] + opened(up_a) + opened(down_a)
    high = home[:, HALF:] + opened(up_b) + opened(down_b)
    rows = CH // (NZ * NC)
    share = packed(jnp.concatenate([low, high], axis=1)).reshape(NZ * NC, rows, KD)
    shares = opened(lax.all_to_all(share, ("z", "c"), 0, 0, tiled=True))
    summed = jnp.sum(shares.reshape(NZ, NC, rows, KD), axis=0)
    return jnp.concatenate([summed[0], summed[1]], axis=1)


def solution(mesh):
    grid = Mesh(mesh.devices.reshape(NZ, NX, NC, NY), ("z", "x", "c", "y"))
    blocks = ("z", "x", "c")
    return jax.shard_map(
        shards,
        mesh=grid,
        in_specs=(P(blocks, None), P("y", None), P()),
        out_specs=P(blocks, "y"),
        check_vma=False,
    )
```

```python
import math

import jax
import jax.numpy as jnp
from jax import lax
from jax.experimental import pallas as pl
from jax.experimental.pallas import tpu as pltpu
from jax.sharding import Mesh, PartitionSpec as P

K = 16384
W = 512
LAG = 5
D = 512
SHARPNESS = 0.03125

NZ, NX, NC, NY = 8, 4, 2, 4
F = 1024
FC = NC * F
TAIL = 128
FE = TAIL + FC
KD = 2048
FB = 256
KB = 256
NB = FC // FB
CH = W // NX
HALF = KD // 2

LOG2E = math.log2(math.e)
DECAY = -SHARPNESS * LOG2E

SENT = jnp.float16
ROOT_SCALE = 8.0


NT = (((1,), (1,)), ((), ()))
VMEM = pl.BlockSpec(memory_space=pltpu.VMEM)
ANY = pl.BlockSpec(memory_space=pl.ANY)


def member_kernel(own, partner, tail_a, tail_b, centers, e_ref, st_ref, peers_ref, xs_out,
                  xs, cs, bias, u0, u1, e0, e1, sems, out_sems):
    c = lax.axis_index("c")
    copies = [
        pltpu.make_async_copy(centers.at[pl.ds(c * KD, KD)], cs, sems.at[0]),
        pltpu.make_async_copy(own, xs.at[pl.ds(TAIL + c * F, F)], sems.at[1]),
        pltpu.make_async_copy(partner, xs.at[pl.ds(TAIL + (1 - c) * F, F)], sems.at[2]),
    ]
    for copy in copies:
        copy.start()
    xs[0:TAIL, :] = tail_a[...] + tail_b[...]
    for copy in copies:
        copy.wait()
    keep_xs = pltpu.make_async_copy(xs, xs_out, sems.at[3])
    keep_xs.start()
    for i in range(KD // KB):
        block = cs[i * KB:(i + 1) * KB, :].astype(jnp.float32)
        norm = jnp.sum(block * block, axis=1, keepdims=True)
        bias[i * KB:(i + 1) * KB, :] = jnp.broadcast_to(norm, (KB, 128))
    slots = (u0, e0), (u1, e1)

    def out_copy(b, slot):
        start = pl.multiple_of(b * FB, FB)
        return pltpu.make_async_copy(slots[slot][1], e_ref.at[:, pl.ds(start, FB)], out_sems.at[slot])

    def stage(new, old):
        if new is not None:
            start, width, slot = new
            u = slots[slot][0]
            xb = xs[pl.ds(start, width), :]
            xf = xb.astype(jnp.float32)
            sq = xf * xf
            part = sq[:, 0:128] + sq[:, 128:256] + sq[:, 256:384] + sq[:, 384:512]
            frame = jnp.sum(part.T, axis=0, keepdims=True)
            twice = xb * jnp.bfloat16(-2.0)
            least = None
        if old is not None:
            start_o, width_o, slot_o, keep, least_o = old
            u_o, e_o = slots[slot_o]
            total = None
        for i in range(KD // KB):
            rows = slice(i * KB, (i + 1) * KB)
            if new is not None:
                ip = lax.dot_general(cs[rows, :], twice, NT, preferred_element_type=jnp.float32)
                b = bias[rows, :]
                v = (frame + ip) + (b if width == 128 else jnp.concatenate([b] * (width // 128), axis=1))
                u[rows, 0:width] = v
                h = jnp.min(v.reshape(KB // 8, 8, width), axis=0)
                least = h if least is None else jnp.minimum(least, h)
            if old is not None:
                e = jnp.exp2((u_o[rows, 0:width_o] - least_o) * DECAY)
                t = jnp.sum(e.reshape(KB // 8, 8, width_o), axis=0)
                total = t if total is None else total + t
                if keep:
                    e_o[rows, :] = e
        if old is not None:
            total = jnp.sum(total, axis=0, keepdims=True)
            both = jnp.concatenate([least_o, total], axis=0)
            peers_ref[:, :, pl.ds(start_o, width_o)] = jnp.broadcast_to(both[None], (NC * NY, 2, width_o))
        if new is not None:
            least = jnp.min(least, axis=0, keepdims=True)
            st_ref[0:1, pl.ds(start, width)] = least
            st_ref[1:2, pl.ds(start, width)] = frame
            return least

    def at(b):
        return pl.multiple_of(TAIL + b * FB, 128)

    least = stage((0, TAIL, 1), None)
    least = stage((TAIL, FB, 0), (0, TAIL, 1, False, least))

    def step(k, least):
        for half in range(2):
            b = 2 * k + half

            @pl.when(k > 0)
            def _():
                out_copy(b - 2, half).wait()

            least = stage((at(b + 1), FB, 1 - half), (at(b), FB, half, True, least))
            out_copy(b, half).start()
        return least

    least = lax.fori_loop(0, NB // 2 - 1, step, least)
    out_copy(NB - 4, 0).wait()
    least = stage((at(NB - 1), FB, 1), (at(NB - 2), FB, 0, True, least))
    out_copy(NB - 2, 0).start()
    out_copy(NB - 3, 1).wait()
    stage(None, (at(NB - 1), FB, 1, True, least))
    out_copy(NB - 1, 1).start()
    out_copy(NB - 2, 0).wait()
    out_copy(NB - 1, 1).wait()
    keep_xs.wait()


def memberships(own, partner, tail_a, tail_b, centers):
    return pl.pallas_call(
        member_kernel,
        in_specs=[ANY, ANY, VMEM, VMEM, ANY],
        out_specs=[ANY, VMEM, VMEM, ANY],
        out_shape=[
            jax.ShapeDtypeStruct((KD, FC), jnp.float32),
            jax.ShapeDtypeStruct((2, FE), jnp.float32),
            jax.ShapeDtypeStruct((NC * NY, 2, FE), jnp.float32),
            jax.ShapeDtypeStruct((FE, D), jnp.bfloat16),
        ],
        scratch_shapes=[
            pltpu.VMEM((FE, D), jnp.bfloat16),
            pltpu.VMEM((KD, D), jnp.bfloat16),
            pltpu.VMEM((KD, 128), jnp.float32),
            pltpu.VMEM((KD, FB), jnp.float32),
            pltpu.VMEM((KD, FB), jnp.float32),
            pltpu.VMEM((KD, FB), jnp.float32),
            pltpu.VMEM((KD, FB), jnp.float32),
            pltpu.SemaphoreType.DMA((4,)),
            pltpu.SemaphoreType.DMA((2,)),
        ],
        cost_estimate=pl.CostEstimate(flops=2 * KD * FE * D, bytes_accessed=2 * (KD * FC + KD * D + FE * D),
                                      transcendentals=KD * FE),
        compiler_params=pltpu.CompilerParams(vmem_limit_bytes=58 * 1024 * 1024),
        name="memberships",
    )(own, partner, tail_a, tail_b, centers)


def window_kernel(near, one, two, three, xs, mine, out, rows, twice, frames, dist, sems):
    x = lax.axis_index("x")
    y = lax.axis_index("y")
    load = pltpu.make_async_copy(xs, frames, sems.at[NX])
    load.start()
    for holder, ref in enumerate((near, one, two, three)):
        @pl.when(y == holder)
        def _():
            for d in range(NX):
                pltpu.make_async_copy(ref.at[:, lax.rem(x + d, NX)], rows.at[d], sems.at[d]).start()

    for d in range(NX):
        pltpu.make_async_copy(near.at[:, 0], rows.at[d], sems.at[d]).wait()
    norms = []
    for d in range(NX):
        part = rows[d].reshape(CH, D)
        pf = part.astype(jnp.float32)
        norms.append(jnp.sum(pf * pf, axis=1, keepdims=True))
        twice[d * CH:(d + 1) * CH, :] = part * jnp.bfloat16(-2.0)
    norm = jnp.concatenate(norms, axis=0)
    load.wait()
    stores = []
    for k, (start, stop) in enumerate(CUTS):
        ip = lax.dot_general(twice[...], frames[start:stop, :], NT, preferred_element_type=jnp.float32)
        dist[:, start:stop] = (mine[1:2, start:stop] + ip) + norm
        stores.append(pltpu.make_async_copy(dist.at[:, start:stop], out.at[:, start:stop], sems.at[NX + 1 + k]))
        stores[-1].start()
    for store in stores:
        store.wait()


CUTS = ((0, 640), (640, 1152), (1152, 1664), (1664, 2176))


def window_distances(windows, xs, mine):
    near, *rest = [w.reshape(NZ, NX, CH // NZ, D) for w in windows]
    windows = [near] + [near_core(w) for w in rest]
    return pl.pallas_call(
        window_kernel,
        in_specs=[ANY] * NY + [ANY, VMEM],
        out_specs=ANY,
        out_shape=jax.ShapeDtypeStruct((W, FE), jnp.float32),
        scratch_shapes=[
            pltpu.VMEM((NX, NZ, CH // NZ, D), jnp.bfloat16),
            pltpu.VMEM((W, D), jnp.bfloat16),
            pltpu.VMEM((FE, D), jnp.bfloat16),
            pltpu.VMEM((W, FE), jnp.float32),
            pltpu.SemaphoreType.DMA((NX + 1 + len(CUTS),)),
        ],
        cost_estimate=pl.CostEstimate(flops=2 * W * FE * D, bytes_accessed=4 * W * FE, transcendentals=0),
        name="window_distances",
    )(*windows, xs, mine)


JB = 512
NJ = KD // JB


def count_kernel(distances, mine, peers, starts, e, edge, pa, mb, home,
                 dist, lead, ebuf, obuf, in_sems, e_sems, out_sems):
    loads = [
        pltpu.make_async_copy(distances.at[pl.ds(d * CH, CH)], dist.at[pl.ds(d * CH, CH)], in_sems.at[d])
        for d in range(NX)
    ]
    e_loads = [
        pltpu.make_async_copy(e.at[pl.ds(b * JB, JB)], ebuf.at[b % 2], e_sems.at[b % 2]) for b in range(NJ)
    ]
    for load in loads + e_loads[:2]:
        load.start()

    mins = peers[:, 0, :]
    least = jnp.min(mins, axis=0, keepdims=True)
    total = jnp.sum(peers[:, 1, :] * jnp.exp2((mins - least) * DECAY), axis=0, keepdims=True)
    inverse = 1.0 / total
    factor = (jnp.exp2((mine[0:1, :] - least) * DECAY) * inverse)[:, TAIL:]
    first = (lax.axis_index("z") * NX + lax.axis_index("x")) * FC
    lag = first - TAIL + lax.broadcasted_iota(jnp.int32, (1, FE), 1)
    n = starts.shape[1]
    square = lax.broadcasted_iota(jnp.int32, (n, n), 0) == lax.broadcasted_iota(jnp.int32, (n, n), 1)
    begin = jnp.sum(jnp.where(square, starts[...].astype(jnp.float32), 0.0), axis=1, keepdims=True).astype(jnp.int32)
    begins = jnp.logical_and(begin <= lag, begin > lag - LAG)
    begun = jnp.sum(jnp.where(begins, 1.0, 0.0), axis=0, keepdims=True)
    usable = jnp.where(jnp.logical_and(begun == 0.0, lag >= LAG), K * K / (NZ * NX * FC), 0.0)
    scale = inverse * pltpu.roll(usable, FE - LAG, 1)

    for d in range(NX):
        loads[d].wait()
        for r in range(d * CH, (d + 1) * CH, 64):
            m = jnp.exp2((dist[r:r + 64, :] - least) * DECAY) * scale
            lead[r:r + 64, :] = pltpu.roll(m, LAG, 1)[:, TAIL:].astype(jnp.bfloat16)

    stores = []
    for b in range(NJ):
        slot = b % 2
        e_loads[b].wait()
        if b >= 2:
            for store in stores[b - 2]:
                store.wait()
        for q in range(0, JB, FB):
            member = (ebuf[slot, q:q + FB, :] * factor).astype(jnp.bfloat16)
            obuf[slot, :, q:q + FB] = lax.dot_general(lead[...], member, NT, preferred_element_type=jnp.float32)
        into = (pa, edge.at[0], edge.at[2]) if b < NJ // 2 else (edge.at[3], edge.at[1], mb)
        at = pl.ds((b % (NJ // 2)) * JB, JB)
        targets = [home.at[:, pl.ds(b * JB, JB)]] + [ref.at[:, at] for ref in into]
        stores.append([
            pltpu.make_async_copy(obuf.at[slot, pl.ds(k * CH, CH)], target, out_sems.at[slot, k])
            for k, target in enumerate(targets)
        ])
        for store in stores[b]:
            store.start()
        if b + 2 < NJ:
            e_loads[b + 2].start()
    for store in stores[NJ - 2] + stores[NJ - 1]:
        store.wait()


def partial_counts(distances, mine, peers, starts, e):
    f32 = jnp.float32
    half = jax.ShapeDtypeStruct((CH, HALF), f32)
    return pl.pallas_call(
        count_kernel,
        in_specs=[ANY] + [VMEM] * 3 + [ANY],
        out_specs=[ANY] * 4,
        out_shape=[jax.ShapeDtypeStruct((4, CH, HALF), f32), half, half, jax.ShapeDtypeStruct((CH, KD), f32)],
        scratch_shapes=[
            pltpu.VMEM((W, FE), f32),
            pltpu.VMEM((W, FC), jnp.bfloat16),
            pltpu.VMEM((2, JB, FC), f32),
            pltpu.VMEM((2, W, JB), f32),
            pltpu.SemaphoreType.DMA((NX,)),
            pltpu.SemaphoreType.DMA((2,)),
            pltpu.SemaphoreType.DMA((2, NX)),
        ],
        cost_estimate=pl.CostEstimate(flops=2 * W * FC * KD, bytes_accessed=4 * FC * KD + 4 * W * FE,
                                      transcendentals=W * FE),
        name="counts",
    )(distances, mine, peers, starts, e)


def near_core(array):
    return pltpu.with_memory_space_constraint(array, pltpu.VMEM)


def along(block, axis, distance):
    n = lax.axis_size(axis)
    return lax.ppermute(block, axis, [(i, (i + distance) % n) for i in range(n)])


def packed(counts):
    return (jnp.sqrt(counts) * ROOT_SCALE).astype(SENT)


def opened(message):
    root = message.astype(jnp.float32) * (1.0 / ROOT_SCALE)
    return root * root


def shards(frames, centers, starts):
    partner = near_core(along(frames, "c", 1))
    last = frames[F - TAIL:]
    blocks = NZ * NX * NC
    chips = ("z", "x", "c")
    tail_a = near_core(lax.ppermute(last, chips, [(i, i + 1) for i in range(1, blocks - 1, 2)]))
    tail_b = near_core(lax.ppermute(last, chips, [(i, i + 2) for i in range(1, blocks - 2, 2)]))
    near = centers[:W]
    windows = [near] + [lax.ppermute(near, "y", [(0, d)]) for d in range(1, NY)]

    e, mine, peers, xs = memberships(frames, partner, tail_a, tail_b, centers)
    peers = near_core(lax.all_to_all(peers, ("c", "y"), 0, 0, tiled=True))
    distances = window_distances(windows, xs, mine)
    edge, pa, mb, home = partial_counts(distances, mine, peers, starts[None, :], e)

    a2, b2, ma, pb = packed(edge)
    via_a = along(a2, "x", 1)
    via_b = along(b2, "x", -1)
    up_b = along(pb, "x", 1)
    down_a = along(ma, "x", -1)
    up_a = along(packed(pa + opened(via_a)), "x", 1)
    down_b = along(packed(mb + opened(via_b)), "x", -1)
    low = home[:, :HALF] + opened(up_a) + opened(down_a)
    high = home[:, HALF:] + opened(up_b) + opened(down_b)
    rows = CH // (NZ * NC)
    share = packed(jnp.concatenate([low, high], axis=1)).reshape(NZ * NC, rows, KD)
    shares = opened(lax.all_to_all(share, ("z", "c"), 0, 0, tiled=True))
    summed = jnp.sum(shares.reshape(NZ, NC, rows, KD), axis=0)
    return jnp.concatenate([summed[0], summed[1]], axis=1)


def solution(mesh):
    grid = Mesh(mesh.devices.reshape(NZ, NX, NC, NY), ("z", "x", "c", "y"))
    blocks = ("z", "x", "c")
    return jax.shard_map(
        shards,
        mesh=grid,
        in_specs=(P(blocks, None), P("y", None), P()),
        out_specs=P(blocks, "y"),
        check_vma=False,
    )
```

```python
import math

import jax
import jax.numpy as jnp
from jax import lax
from jax.experimental import pallas as pl
from jax.experimental.pallas import tpu as pltpu
from jax.sharding import Mesh, PartitionSpec as P

K = 16384
W = 512
LAG = 5
D = 512
SHARPNESS = 0.03125

NZ, NX, NC, NY = 8, 4, 2, 4
F = 1024
FC = NC * F
TAIL = 128
FE = TAIL + FC
KD = 2048
FB = 256
KB = 256
NB = FC // FB
CH = W // NX
HALF = KD // 2

LOG2E = math.log2(math.e)
DECAY = -SHARPNESS * LOG2E

SENT = jnp.float16
ROOT_SCALE = 8.0


NT = (((1,), (1,)), ((), ()))
VMEM = pl.BlockSpec(memory_space=pltpu.VMEM)
ANY = pl.BlockSpec(memory_space=pl.ANY)


def member_kernel(own, partner, tail_a, tail_b, centers, e_ref, st_ref, peers_ref, xs_out,
                  xs, cs, bias, u0, u1, e0, e1, sems, out_sems):
    c = lax.axis_index("c")
    quarter = KD // 4
    copies = [
        pltpu.make_async_copy(centers.at[pl.ds(c * KD + q * quarter, quarter)], cs.at[pl.ds(q * quarter, quarter)], sems.at[q])
        for q in range(4)
    ] + [
        pltpu.make_async_copy(own, xs.at[pl.ds(TAIL + c * F, F)], sems.at[4]),
        pltpu.make_async_copy(partner, xs.at[pl.ds(TAIL + (1 - c) * F, F)], sems.at[5]),
    ]
    for copy in copies:
        copy.start()
    xs[0:TAIL, :] = tail_a[...] + tail_b[...]
    for i in range(KD // KB):
        if i * KB % quarter == 0:
            copies[i * KB // quarter].wait()
        block = cs[i * KB:(i + 1) * KB, :].astype(jnp.float32)
        norm = jnp.sum(block * block, axis=1, keepdims=True)
        bias[i * KB:(i + 1) * KB, :] = jnp.broadcast_to(norm, (KB, 128))
    for copy in copies[4:]:
        copy.wait()
    keep_xs = pltpu.make_async_copy(xs, xs_out, sems.at[6])
    keep_xs.start()
    slots = (u0, e0), (u1, e1)

    def out_copy(b, slot):
        start = pl.multiple_of(b * FB, FB)
        return pltpu.make_async_copy(slots[slot][1], e_ref.at[:, pl.ds(start, FB)], out_sems.at[slot])

    def stage(new, old):
        if new is not None:
            start, width, slot = new
            u = slots[slot][0]
            xb = xs[pl.ds(start, width), :]
            xf = xb.astype(jnp.float32)
            sq = xf * xf
            part = sq[:, 0:128] + sq[:, 128:256] + sq[:, 256:384] + sq[:, 384:512]
            frame = jnp.sum(part.T, axis=0, keepdims=True)
            twice = xb * jnp.bfloat16(-2.0)
            least = None
        if old is not None:
            start_o, width_o, slot_o, keep, least_o = old
            u_o, e_o = slots[slot_o]
            total = None
        for i in range(KD // KB):
            rows = slice(i * KB, (i + 1) * KB)
            if new is not None:
                ip = lax.dot_general(cs[rows, :], twice, NT, preferred_element_type=jnp.float32)
                b = bias[rows, :]
                v = (frame + ip) + (b if width == 128 else jnp.concatenate([b] * (width // 128), axis=1))
                u[rows, 0:width] = v
                h = jnp.min(v.reshape(KB // 8, 8, width), axis=0)
                least = h if least is None else jnp.minimum(least, h)
            if old is not None:
                e = jnp.exp2((u_o[rows, 0:width_o] - least_o) * DECAY)
                t = jnp.sum(e.reshape(KB // 8, 8, width_o), axis=0)
                total = t if total is None else total + t
                if keep:
                    e_o[rows, :] = e
        if old is not None:
            total = jnp.sum(total, axis=0, keepdims=True)
            both = jnp.concatenate([least_o, total], axis=0)
            peers_ref[:, :, pl.ds(start_o, width_o)] = jnp.broadcast_to(both[None], (NC * NY, 2, width_o))
        if new is not None:
            least = jnp.min(least, axis=0, keepdims=True)
            st_ref[0:1, pl.ds(start, width)] = least
            st_ref[1:2, pl.ds(start, width)] = frame
            return least

    def at(b):
        return pl.multiple_of(TAIL + b * FB, 128)

    least = stage((0, TAIL, 1), None)
    least = stage((TAIL, FB, 0), (0, TAIL, 1, False, least))

    def step(k, least):
        for half in range(2):
            b = 2 * k + half

            @pl.when(k > 0)
            def _():
                out_copy(b - 2, half).wait()

            least = stage((at(b + 1), FB, 1 - half), (at(b), FB, half, True, least))
            out_copy(b, half).start()
        return least

    least = lax.fori_loop(0, NB // 2 - 1, step, least)
    out_copy(NB - 4, 0).wait()
    least = stage((at(NB - 1), FB, 1), (at(NB - 2), FB, 0, True, least))
    out_copy(NB - 2, 0).start()
    out_copy(NB - 3, 1).wait()
    stage(None, (at(NB - 1), FB, 1, True, least))
    out_copy(NB - 1, 1).start()
    out_copy(NB - 2, 0).wait()
    out_copy(NB - 1, 1).wait()
    keep_xs.wait()


def memberships(own, partner, tail_a, tail_b, centers):
    return pl.pallas_call(
        member_kernel,
        in_specs=[ANY, ANY, VMEM, VMEM, ANY],
        out_specs=[ANY, VMEM, VMEM, ANY],
        out_shape=[
            jax.ShapeDtypeStruct((KD, FC), jnp.float32),
            jax.ShapeDtypeStruct((2, FE), jnp.float32),
            jax.ShapeDtypeStruct((NC * NY, 2, FE), jnp.float32),
            jax.ShapeDtypeStruct((FE, D), jnp.bfloat16),
        ],
        scratch_shapes=[
            pltpu.VMEM((FE, D), jnp.bfloat16),
            pltpu.VMEM((KD, D), jnp.bfloat16),
            pltpu.VMEM((KD, 128), jnp.float32),
            pltpu.VMEM((KD, FB), jnp.float32),
            pltpu.VMEM((KD, FB), jnp.float32),
            pltpu.VMEM((KD, FB), jnp.float32),
            pltpu.VMEM((KD, FB), jnp.float32),
            pltpu.SemaphoreType.DMA((7,)),
            pltpu.SemaphoreType.DMA((2,)),
        ],
        cost_estimate=pl.CostEstimate(flops=2 * KD * FE * D, bytes_accessed=2 * (KD * FC + KD * D + FE * D),
                                      transcendentals=KD * FE),
        compiler_params=pltpu.CompilerParams(vmem_limit_bytes=58 * 1024 * 1024),
        name="memberships",
    )(own, partner, tail_a, tail_b, centers)


def window_kernel(near, one, two, three, xs, mine, out, rows, twice, frames, dist, sems):
    x = lax.axis_index("x")
    y = lax.axis_index("y")
    load = pltpu.make_async_copy(xs, frames, sems.at[NX])
    load.start()
    for holder, ref in enumerate((near, one, two, three)):
        @pl.when(y == holder)
        def _():
            for d in range(NX):
                pltpu.make_async_copy(ref.at[:, lax.rem(x + d, NX)], rows.at[d], sems.at[d]).start()

    for d in range(NX):
        pltpu.make_async_copy(near.at[:, 0], rows.at[d], sems.at[d]).wait()
    norms = []
    for d in range(NX):
        part = rows[d].reshape(CH, D)
        pf = part.astype(jnp.float32)
        norms.append(jnp.sum(pf * pf, axis=1, keepdims=True))
        twice[d * CH:(d + 1) * CH, :] = part * jnp.bfloat16(-2.0)
    norm = jnp.concatenate(norms, axis=0)
    load.wait()
    stores = []
    for k, (start, stop) in enumerate(CUTS):
        ip = lax.dot_general(twice[...], frames[start:stop, :], NT, preferred_element_type=jnp.float32)
        dist[:, start:stop] = (mine[1:2, start:stop] + ip) + norm
        stores.append(pltpu.make_async_copy(dist.at[:, start:stop], out.at[:, start:stop], sems.at[NX + 1 + k]))
        stores[-1].start()
    for store in stores:
        store.wait()


CUTS = ((0, 640), (640, 1152), (1152, 1664), (1664, 2176))


def window_distances(windows, xs, mine):
    near, *rest = [w.reshape(NZ, NX, CH // NZ, D) for w in windows]
    windows = [near] + [near_core(w) for w in rest]
    return pl.pallas_call(
        window_kernel,
        in_specs=[ANY] * NY + [ANY, VMEM],
        out_specs=ANY,
        out_shape=jax.ShapeDtypeStruct((W, FE), jnp.float32),
        scratch_shapes=[
            pltpu.VMEM((NX, NZ, CH // NZ, D), jnp.bfloat16),
            pltpu.VMEM((W, D), jnp.bfloat16),
            pltpu.VMEM((FE, D), jnp.bfloat16),
            pltpu.VMEM((W, FE), jnp.float32),
            pltpu.SemaphoreType.DMA((NX + 1 + len(CUTS),)),
        ],
        cost_estimate=pl.CostEstimate(flops=2 * W * FE * D, bytes_accessed=4 * W * FE, transcendentals=0),
        name="window_distances",
    )(*windows, xs, mine)


JB = 512
NJ = KD // JB


def count_kernel(distances, mine, peers, starts, e, edge, pa, mb, home,
                 dist, lead, ebuf, obuf, in_sems, e_sems, out_sems):
    loads = [
        pltpu.make_async_copy(distances.at[pl.ds(d * CH, CH)], dist.at[pl.ds(d * CH, CH)], in_sems.at[d])
        for d in range(NX)
    ]
    e_loads = [
        pltpu.make_async_copy(e.at[pl.ds(b * JB, JB)], ebuf.at[b % 2], e_sems.at[b % 2]) for b in range(NJ)
    ]
    for load in loads + e_loads[:2]:
        load.start()

    mins = peers[:, 0, :]
    least = jnp.min(mins, axis=0, keepdims=True)
    total = jnp.sum(peers[:, 1, :] * jnp.exp2((mins - least) * DECAY), axis=0, keepdims=True)
    inverse = 1.0 / total
    factor = (jnp.exp2((mine[0:1, :] - least) * DECAY) * inverse)[:, TAIL:]
    first = (lax.axis_index("z") * NX + lax.axis_index("x")) * FC
    lag = first - TAIL + lax.broadcasted_iota(jnp.int32, (1, FE), 1)
    n = starts.shape[1]
    square = lax.broadcasted_iota(jnp.int32, (n, n), 0) == lax.broadcasted_iota(jnp.int32, (n, n), 1)
    begin = jnp.sum(jnp.where(square, starts[...].astype(jnp.float32), 0.0), axis=1, keepdims=True).astype(jnp.int32)
    begins = jnp.logical_and(begin <= lag, begin > lag - LAG)
    begun = jnp.sum(jnp.where(begins, 1.0, 0.0), axis=0, keepdims=True)
    usable = jnp.where(jnp.logical_and(begun == 0.0, lag >= LAG), K * K / (NZ * NX * FC), 0.0)
    scale = inverse * pltpu.roll(usable, FE - LAG, 1)

    for d in range(NX):
        loads[d].wait()
        for r in range(d * CH, (d + 1) * CH, 64):
            m = jnp.exp2((dist[r:r + 64, :] - least) * DECAY) * scale
            lead[r:r + 64, :] = pltpu.roll(m, LAG, 1)[:, TAIL:].astype(jnp.bfloat16)

    stores = []
    for b in range(NJ):
        slot = b % 2
        e_loads[b].wait()
        if b >= 2:
            for store in stores[b - 2]:
                store.wait()
        for q in range(0, JB, FB):
            member = (ebuf[slot, q:q + FB, :] * factor).astype(jnp.bfloat16)
            obuf[slot, :, q:q + FB] = lax.dot_general(lead[...], member, NT, preferred_element_type=jnp.float32)
        into = (pa, edge.at[0], edge.at[2]) if b < NJ // 2 else (edge.at[3], edge.at[1], mb)
        at = pl.ds((b % (NJ // 2)) * JB, JB)
        targets = [home.at[:, pl.ds(b * JB, JB)]] + [ref.at[:, at] for ref in into]
        stores.append([
            pltpu.make_async_copy(obuf.at[slot, pl.ds(k * CH, CH)], target, out_sems.at[slot, k])
            for k, target in enumerate(targets)
        ])
        for store in stores[b]:
            store.start()
        if b + 2 < NJ:
            e_loads[b + 2].start()
    for store in stores[NJ - 2] + stores[NJ - 1]:
        store.wait()


def partial_counts(distances, mine, peers, starts, e):
    f32 = jnp.float32
    half = jax.ShapeDtypeStruct((CH, HALF), f32)
    return pl.pallas_call(
        count_kernel,
        in_specs=[ANY] + [VMEM] * 3 + [ANY],
        out_specs=[ANY] * 4,
        out_shape=[jax.ShapeDtypeStruct((4, CH, HALF), f32), half, half, jax.ShapeDtypeStruct((CH, KD), f32)],
        scratch_shapes=[
            pltpu.VMEM((W, FE), f32),
            pltpu.VMEM((W, FC), jnp.bfloat16),
            pltpu.VMEM((2, JB, FC), f32),
            pltpu.VMEM((2, W, JB), f32),
            pltpu.SemaphoreType.DMA((NX,)),
            pltpu.SemaphoreType.DMA((2,)),
            pltpu.SemaphoreType.DMA((2, NX)),
        ],
        cost_estimate=pl.CostEstimate(flops=2 * W * FC * KD, bytes_accessed=4 * FC * KD + 4 * W * FE,
                                      transcendentals=W * FE),
        name="counts",
    )(distances, mine, peers, starts, e)


def near_core(array):
    return pltpu.with_memory_space_constraint(array, pltpu.VMEM)


def along(block, axis, distance):
    n = lax.axis_size(axis)
    return lax.ppermute(block, axis, [(i, (i + distance) % n) for i in range(n)])


def packed(counts):
    return (jnp.sqrt(counts) * ROOT_SCALE).astype(SENT)


def opened(message):
    root = message.astype(jnp.float32) * (1.0 / ROOT_SCALE)
    return root * root


def shards(frames, centers, starts):
    partner = near_core(along(frames, "c", 1))
    last = frames[F - TAIL:]
    blocks = NZ * NX * NC
    chips = ("z", "x", "c")
    tail_a = near_core(lax.ppermute(last, chips, [(i, i + 1) for i in range(1, blocks - 1, 2)]))
    tail_b = near_core(lax.ppermute(last, chips, [(i, i + 2) for i in range(1, blocks - 2, 2)]))
    near = centers[:W]
    windows = [near] + [lax.ppermute(near, "y", [(0, d)]) for d in range(1, NY)]

    e, mine, peers, xs = memberships(frames, partner, tail_a, tail_b, centers)
    peers = near_core(lax.all_to_all(peers, ("c", "y"), 0, 0, tiled=True))
    distances = window_distances(windows, xs, mine)
    edge, pa, mb, home = partial_counts(distances, mine, peers, starts[None, :], e)

    a2, b2, ma, pb = packed(edge)
    via_a = along(a2, "x", 1)
    via_b = along(b2, "x", -1)
    up_b = along(pb, "x", 1)
    down_a = along(ma, "x", -1)
    up_a = along(packed(pa + opened(via_a)), "x", 1)
    down_b = along(packed(mb + opened(via_b)), "x", -1)
    low = home[:, :HALF] + opened(up_a) + opened(down_a)
    high = home[:, HALF:] + opened(up_b) + opened(down_b)
    rows = CH // (NZ * NC)
    share = packed(jnp.concatenate([low, high], axis=1)).reshape(NZ * NC, rows, KD)
    shares = opened(lax.all_to_all(share, ("z", "c"), 0, 0, tiled=True))
    summed = jnp.sum(shares.reshape(NZ, NC, rows, KD), axis=0)
    return jnp.concatenate([summed[0], summed[1]], axis=1)


def solution(mesh):
    grid = Mesh(mesh.devices.reshape(NZ, NX, NC, NY), ("z", "x", "c", "y"))
    blocks = ("z", "x", "c")
    return jax.shard_map(
        shards,
        mesh=grid,
        in_specs=(P(blocks, None), P("y", None), P()),
        out_specs=P(blocks, "y"),
        check_vma=False,
    )
```
